32 devices in a mesh: tm: 4 (over y, x), gx: 8 (over z, core).
Axes of the slice: x: 2, y: 2, z: 4, core: 2. Of those that a mesh axis runs over, the one named last changes fastest.
Arguments:
- state: float32 [8, 32, 256, 128], P('tm', 'gx'), may hold values from -3 to 3
- start_field: float32 [32, 256, 128], P('gx'), may hold values from -3 to 3
- diffusivity: float32 [32, 256, 128], P('gx'), may hold values from 0.3 to 3
- time_weights: float32 [8], P('tm'), may hold values from 0.4 to 1
- shift_real: float32 [8], replicated, may hold values from 0.5 to 2, as said below
- shift_imag: float32 [8], replicated, may hold values from -1 to 1, as said below
Outputs:
- new_state: float32 [8, 32, 256, 128], P('tm', 'gx')
The draws below stay inside these ranges and needn't reach their ends.
Inputs may be any that keep to these rules, and one draw needn't show every extreme that they name: `shift_real`: shift_real_k = shift_real_(8 - k) for k = 1 .. 7. `shift_imag`: shift_imag_0 = shift_imag_(4) = 0 and shift_imag_k = - shift_imag_(8 - k), so the eigenvalues come in conjugate pairs.
All inputs are finite; a program needn't handle non-finite values.
Results may differ from the reference program's by a relative error of at most 0.0003.
Values sent between devices are 32-bit elements; how exact they have to be, the bound alone decides.
No kernel may reach another device: no remote copies, remote signals or barrier semaphores. Data moves between devices by JAX's collectives and lax.ppermute only.
A program may use at most 64 MiB of HBM per device.

```python
import math
import jax
import jax.numpy as jnp
from jax import lax

STEPS = 8
CY = 256
CZ = 128
SWEEPS = 12
NX = 32


def folded_modes():
    position = jnp.arange(STEPS)
    return (position, jnp.minimum(position, STEPS - position))


def draw_shift_real(key, part):
    half_count = STEPS // 2 + 1
    base_values = jnp.exp(jax.random.uniform(jax.random.fold_in(key, 11), (half_count,), jnp.float32, math.log(0.5), math.log(2.0)))
    position, folded = folded_modes()
    return base_values[folded].astype(jnp.float32)


def draw_shift_imag(key, part):
    half_count = STEPS // 2 + 1
    base_values = jax.random.uniform(jax.random.fold_in(key, 23), (half_count,), jnp.float32, -1.0, 1.0)
    position, folded = folded_modes()
    flipped = jnp.where(position > STEPS // 2, -1.0, 1.0).astype(jnp.float32)
    inside = (folded > 0) & (folded < STEPS // 2)
    return jnp.where(inside, base_values[folded] * flipped, 0.0).astype(jnp.float32)


def shard_levels(key, shape, pieces, smallest, high):
    def one(dim, blocks):
        draws = jax.random.uniform(jax.random.fold_in(jax.random.fold_in(key, 6), dim), (blocks,), jnp.float32, smallest / len(pieces), high / len(pieces))
        return jnp.repeat(jnp.exp(draws), shape[dim] // blocks).reshape((-1,) + (1,) * (len(shape) - dim - 1))

    loudness = one(*pieces[0])
    for cut in pieces[1:]:
        loudness = loudness * one(*cut)
    return loudness


def noise(key, shape, deviation, limit, pieces=(), dtype=jnp.bfloat16):
    entries = jax.random.normal(key, shape, jnp.float32) * deviation
    if len(pieces) > 0:
        entries = shard_levels(key, shape, pieces, -0.22, 0.18) * entries
    return jnp.clip(entries, min=-limit, max=limit).astype(dtype)


def setup_inputs(seed: int = 0) -> dict:
    streams_of = jax.random.split(jax.random.key(seed), 7)
    return {
        "state": noise(streams_of[0], (STEPS, NX, CY, CZ), 0.5, 3.0, ((0, 4), (1, 8)), jnp.float32),
        "start_field": noise(streams_of[1], (NX, CY, CZ), 0.5, 3.0, ((0, 8),), jnp.float32),
        "diffusivity": jnp.clip(jnp.exp(math.log(3.0) - 2.3025851 * jax.random.uniform(streams_of[2], (NX, CY, CZ), jnp.float32) ** shard_levels(streams_of[2], (NX, CY, CZ), ((0, 8),), -0.2, 0.2)), 0.3, 3.0),
        "time_weights": jnp.clip(jnp.exp(math.log(1.0) - 0.9162907 * jax.random.uniform(streams_of[3], (STEPS,), jnp.float32) ** shard_levels(streams_of[3], (STEPS,), ((0, 4),), -0.2, 0.2)), 0.4, 1.0),
        "shift_real": draw_shift_real(jax.random.fold_in(streams_of[6], 71), 0),
        "shift_imag": draw_shift_imag(jax.random.fold_in(streams_of[6], 71), 0),
    }


cheb_centre = 1.0
cheb_half = 0.7


def along(core, axis, lower):
    length = core.shape[axis]
    zeros = jnp.zeros_like(lax.slice_in_dim(core, 0, 1, axis=axis))
    if lower:
        return jnp.concatenate([zeros, lax.slice_in_dim(core, 0, length - 1, axis=axis)], axis)
    return jnp.concatenate([lax.slice_in_dim(core, 1, length, axis=axis), zeros], axis)


def six_near(padded):
    core = padded[..., 1:-1, :, :]
    rank = core.ndim
    return core, (padded[..., :-2, :, :], padded[..., 2:, :, :], along(core, rank - 2, True), along(core, rank - 2, False), along(core, rank - 1, True), along(core, rank - 1, False))


def operate(padded, faces, diag_sum):
    core, near = six_near(padded)
    total = faces[0] * near[0]
    for which in range(1, 6):
        total = total + faces[which] * near[which]
    return diag_sum * core - total


def pad_first(field):
    return jnp.pad(field, ((1, 1), (0, 0), (0, 0)))


def reference(state, start_field, diffusivity, time_weights, shift_real, shift_imag):
    kappa, near = six_near(pad_first(diffusivity))
    faces = [0.5 * (kappa + other) for other in near]
    diag_sum = faces[0]
    for which in range(1, 6):
        diag_sum = diag_sum + faces[which]
    prior = jnp.concatenate([start_field[None], state[:-1]], 0)

    def react(pair):
        now, before = pair
        applied = operate(pad_first(now), faces, diag_sum)
        return before - now - (applied + now * now * now - now)

    residual = lax.map(react, (state, prior))
    spectrum = jnp.fft.fft(time_weights[:, None, None, None] * residual, axis=0)

    def solve(inputs):
        source_real, source_imag, mode_real, mode_imag = inputs
        denom_real = mode_real + diag_sum
        magnitude = denom_real * denom_real + mode_imag * mode_imag
        inverse_real = denom_real / magnitude
        inverse_imag = -mode_imag / magnitude
        answer_real = source_real * inverse_real - source_imag * inverse_imag
        answer_imag = source_real * inverse_imag + source_imag * inverse_real
        for turn in range(SWEEPS):
            omega = 1.0 / (cheb_centre + cheb_half * math.cos(math.pi * (2 * turn + 1) / (2 * SWEEPS)))
            applied_real = operate(pad_first(answer_real), faces, diag_sum)
            applied_imag = operate(pad_first(answer_imag), faces, diag_sum)
            misfit_real = source_real - (mode_real * answer_real - mode_imag * answer_imag + applied_real)
            misfit_imag = source_imag - (mode_real * answer_imag + mode_imag * answer_real + applied_imag)
            answer_real = answer_real + omega * (misfit_real * inverse_real - misfit_imag * inverse_imag)
            answer_imag = answer_imag + omega * (misfit_real * inverse_imag + misfit_imag * inverse_real)
        return answer_real, answer_imag

    answer_real, answer_imag = lax.map(solve, (jnp.real(spectrum), jnp.imag(spectrum), shift_real, shift_imag))
    back = jnp.fft.ifft(answer_real + 1j * answer_imag, axis=0)
    return state + jnp.real(back) / time_weights[:, None, None, None]
```

```python
import functools
import math

import jax
import jax.numpy as jnp
import numpy as np
from jax import lax
from jax.experimental import pallas as pl
from jax.experimental.pallas import tpu as pltpu
from jax.sharding import PartitionSpec as P

SWEEPS = 12
DEPTH = 3
YHALO = 16
PAD = 8
GROUPS = 1

cheb_centre = 1.0
cheb_half = 0.7

VMEM = pl.BlockSpec(memory_space=pltpu.VMEM)
SMEM = pl.BlockSpec(memory_space=pltpu.SMEM)


def omegas():
    return [
        1.0
        / (cheb_centre + cheb_half * math.cos(math.pi * (2 * turn + 1) / (2 * SWEEPS)))
        for turn in range(SWEEPS)
    ]


def forward_table(total):
    time = np.arange(total)
    table = np.zeros((total, total))
    table[0] = 1.0
    table[1] = np.where(time % 2 == 0, 1.0, -1.0)
    for mode in range(1, total // 2):
        angle = 2.0 * np.pi * (mode * time % total) / total
        table[2 * mode] = np.cos(angle)
        table[2 * mode + 1] = -np.sin(angle)
    return table


def inverse_table(total):
    table = forward_table(total).T.copy()
    table[:, 2:] *= 2.0
    return table / total


def near_sum(w_ref, lead, coef_ref, plane, row, rows=8):
    lanes = w_ref.shape[-1]
    at = pl.ds(row, rows)
    below = pl.ds(row - 1, rows)
    above = pl.ds(row + 1, rows)
    core = w_ref[lead, plane, at, :]
    face = coef_ref[2, plane, at, :]
    total = coef_ref[0, plane, at, :] * w_ref[lead, plane - 1, at, :]
    total = total + coef_ref[0, plane + 1, at, :] * w_ref[lead, plane + 1, at, :]
    total = total + coef_ref[1, plane, at, :] * w_ref[lead, plane, below, :]
    total = total + coef_ref[1, plane, above, :] * w_ref[lead, plane, above, :]
    total = total + face * pltpu.roll(core, 1, 1)
    total = total + pltpu.roll(face * core, lanes - 1, 1)
    return core, total


def sweeps_on(buffers, coef_ref, w0_ref, inv_ref, first, block, chunks, w0_plane, w0_row):
    own = DEPTH + 1
    for step in range(DEPTH):
        omega = omegas()[first + step]
        source, target = buffers[step % 2], buffers[(step + 1) % 2]
        reach = DEPTH - 1 - step

        def one(plane, _):
            for chunk in chunks:
                row = PAD + 8 * chunk
                at = pl.ds(8 * chunk - w0_row, 8)
                core_a, sum_a = near_sum(source, 0, coef_ref, plane, row)
                core_b, sum_b = near_sum(source, 1, coef_ref, plane, row)
                cross = inv_ref[2, plane - w0_plane, at, :]
                term_a = inv_ref[0, plane - w0_plane, at, :] * sum_a - cross * sum_b
                term_b = inv_ref[1, plane - w0_plane, at, :] * sum_b + cross * sum_a
                target[0, plane, pl.ds(row, 8), :] = (1.0 - omega) * core_a + omega * (
                    w0_ref[0, plane - w0_plane, at, :] + term_a
                )
                target[1, plane, pl.ds(row, 8), :] = (1.0 - omega) * core_b + omega * (
                    w0_ref[1, plane - w0_plane, at, :] + term_b
                )
            return 0

        lax.fori_loop(own - reach, own + block + reach, one, 0)
    return buffers[DEPTH % 2]


def send_out(result, parity, own_ref, on_ref, off_ref, block, window):
    low, rows = window
    own = DEPTH + 1
    first_on = jnp.where(parity == 0, block - DEPTH, 0)
    first_off = jnp.where(parity == 0, 0, block - DEPTH)
    for which in range(2):
        for plane in range(block):
            own_ref[which, plane] = result[which, own + plane, pl.ds(PAD + low, rows), :]
        for plane in range(DEPTH):
            on_ref[which, plane] = result[which, own + first_on + plane, pl.ds(PAD + low, rows), :]
            off_ref[which, plane] = result[which, own + first_off + plane, pl.ds(PAD + low, rows), :]


def pack_kernel(chunk, weights_ref, state_ref, out_ref):
    step, plane = pl.program_id(0), pl.program_id(1)
    pieces, rows, lanes = out_ref.shape[0], out_ref.shape[3], out_ref.shape[4]
    length = state_ref.shape[2]
    for piece in range(pieces):
        low = piece * chunk - YHALO
        first, last = max(low, 0), min(low + rows, length)
        if first > low:
            out_ref[piece, 0, 0, pl.ds(0, first - low), :] = jnp.zeros((first - low, lanes), jnp.float32)
        if last < low + rows:
            out_ref[piece, 0, 0, pl.ds(last - low, low + rows - last), :] = jnp.zeros(
                (low + rows - last, lanes), jnp.float32
            )
        out_ref[piece, 0, 0, pl.ds(first - low, last - first), :] = state_ref[
            0, 0, pl.ds(first, last - first), :
        ]

    @pl.when(plane == 0)
    def _():
        for piece in range(pieces):
            out_ref[piece, 0, 0, pl.ds(0, 1), :] = jnp.full((1, lanes), weights_ref[step], jnp.float32)


def finish_kernel(total, weights_ref, state_ref, back_ref, out_ref):
    step = pl.program_id(0)
    pieces, chunk = back_ref.shape[0], back_ref.shape[3]
    weight = jnp.full((8, state_ref.shape[3]), weights_ref[step], jnp.float32)
    scale = (1.0 / weight)[:1]
    for piece in range(pieces):
        at = pl.ds(piece * chunk, chunk)
        out_ref[0, 0, at, :] = state_ref[0, 0, at, :] + back_ref[piece, 0, 0] * scale


def setup_kernel(
    window,
    parity_ref,
    table_ref,
    shift_real_ref,
    shift_imag_ref,
    state_own,
    state_on,
    state_off,
    fixed_own,
    fixed_on,
    fixed_off,
    own_ref,
    on_ref,
    off_ref,
    w0_ref,
    inv_ref,
    coef_ref,
    wide,
    fixed,
    diag,
    resid,
    start,
    inverse,
    buffer_a,
    buffer_b,
):
    pair = pl.program_id(0)
    total, block, rows, lanes = state_own.shape
    own = DEPTH + 1
    planes = block + 2 * own
    padded = rows + 2 * PAD
    parity = parity_ref[0]
    chunks = range(rows // 8)

    @pl.when(pair == 0)
    def _():
        first_on = jnp.where(parity == 0, own + block, 0)
        first_off = jnp.where(parity == 0, 0, own + block)
        blank = jnp.zeros((PAD, lanes), jnp.float32)

        def clear(plane, _):
            for ref in (wide, fixed, coef_ref, buffer_a, buffer_b):
                for lead in range(ref.shape[0]):
                    ref[lead, plane, pl.ds(0, PAD), :] = blank
                    ref[lead, plane, pl.ds(padded - PAD, PAD), :] = blank
            return 0

        lax.fori_loop(0, planes, clear, 0)
        body = pl.ds(PAD, rows)

        def place(plane, _):
            for lead in range(total):
                wide[lead, own + plane, body, :] = state_own[lead, plane]
                wide[lead, first_on + plane, body, :] = state_on[lead, plane]
                wide[lead, first_off + plane, body, :] = state_off[lead, plane]
            for lead in range(2):
                fixed[lead, own + plane, body, :] = fixed_own[lead, plane]
                fixed[lead, first_on + plane, body, :] = fixed_on[lead, plane]
                fixed[lead, first_off + plane, body, :] = fixed_off[lead, plane]
            return 0

        lax.fori_loop(0, block, place, 0)
        lane = lax.broadcasted_iota(jnp.int32, (8, lanes), 1)

        def faces(plane, _):
            for chunk in chunks:
                row = PAD + 8 * chunk
                at = pl.ds(row, 8)
                kappa = fixed[1, plane, at, :]
                coef_ref[0, plane, at, :] = 0.5 * (fixed[1, plane - 1, at, :] + kappa)
                coef_ref[1, plane, at, :] = 0.5 * (fixed[1, plane, pl.ds(row - 1, 8), :] + kappa)
                near = 0.5 * (pltpu.roll(kappa, 1, 1) + kappa)
                coef_ref[2, plane, at, :] = jnp.where(lane == 0, 0.0, near)
            return 0

        lax.fori_loop(1, planes, faces, 0)

        def residuals(plane, _):
            for chunk in chunks:
                row = PAD + 8 * chunk
                at = pl.ds(row, 8)
                kappa = fixed[1, plane, at, :]
                low = 0.5 * (kappa + jnp.where(lane == 0, 0.0, pltpu.roll(kappa, 1, 1)))
                high = 0.5 * (kappa + jnp.where(lane == lanes - 1, 0.0, pltpu.roll(kappa, lanes - 1, 1)))
                around = coef_ref[0, plane, at, :] + coef_ref[0, plane + 1, at, :]
                around = around + coef_ref[1, plane, at, :]
                around = around + coef_ref[1, plane, pl.ds(row + 1, 8), :]
                around = around + low + high
                diag[plane, pl.ds(8 * chunk, 8), :] = around
                for lead in range(total):
                    core, near = near_sum(wide, lead, coef_ref, plane, row)
                    if lead == 0:
                        prior = fixed[0, plane, at, :]
                    else:
                        prior = wide[lead - 1, plane, at, :]
                    value = prior - (around * core - near) - core * core * core
                    weight = state_own[lead, 0, pl.ds(0, 1), :]
                    resid[lead, plane, pl.ds(8 * chunk, 8), :] = value * weight
            return 0

        lax.fori_loop(1, planes - 1, residuals, 0)

    other = jnp.where(pair == 0, total // 2, pair)
    real_a = shift_real_ref[pair]
    real_b = shift_real_ref[other]
    imag = shift_imag_ref[pair]
    table_a = [table_ref[2 * pair, lead] for lead in range(total)]
    table_b = [table_ref[2 * pair + 1, lead] for lead in range(total)]

    def begin(plane, _):
        for chunk in chunks:
            at = pl.ds(8 * chunk, 8)
            inside = fixed[1, plane, pl.ds(PAD + 8 * chunk, 8), :] > 0.0
            around = diag[plane, at, :]
            denom_a = real_a + around
            denom_b = real_b + around
            scale_a = 1.0 / (denom_a * denom_a + imag * imag)
            scale_b = 1.0 / (denom_b * denom_b + imag * imag)
            inv_a = jnp.where(inside, denom_a * scale_a, 0.0)
            inv_b = jnp.where(inside, denom_b * scale_b, 0.0)
            cross = jnp.where(inside, -imag * scale_a, 0.0)
            value = resid[0, plane, at, :]
            spec_a = table_a[0] * value
            spec_b = table_b[0] * value
            for lead in range(1, total):
                value = resid[lead, plane, at, :]
                spec_a = spec_a + table_a[lead] * value
                spec_b = spec_b + table_b[lead] * value
            w_a = inv_a * spec_a - cross * spec_b
            w_b = inv_b * spec_b + cross * spec_a
            inverse[0, plane, at, :] = inv_a
            inverse[1, plane, at, :] = inv_b
            inverse[2, plane, at, :] = cross
            start[0, plane, at, :] = w_a
            start[1, plane, at, :] = w_b
            buffer_a[0, plane, pl.ds(PAD + 8 * chunk, 8), :] = w_a
            buffer_a[1, plane, pl.ds(PAD + 8 * chunk, 8), :] = w_b
        return 0

    lax.fori_loop(1, planes - 1, begin, 0)
    result = sweeps_on((buffer_a, buffer_b), coef_ref, start, inverse, 0, block, chunks, 0, 0)
    send_out(result, parity, own_ref, on_ref, off_ref, block, window)

    def keep(plane, _):
        for lead in range(2):
            w0_ref[lead, plane] = start[lead, plane + 2, pl.ds(8, rows - 16), :]
        for lead in range(3):
            inv_ref[lead, plane] = inverse[lead, plane + 2, pl.ds(8, rows - 16), :]
        return 0

    lax.fori_loop(0, planes - 4, keep, 0)


def load_in(parity, own_ref, on_ref, off_ref, buffer_a, block, window):
    low, rows = window
    own = DEPTH + 1
    at = pl.ds(PAD + low, rows)
    first_on = jnp.where(parity == 0, own + block, 1)
    first_off = jnp.where(parity == 0, 1, own + block)
    for which in range(2):
        for plane in range(block):
            buffer_a[which, own + plane, at, :] = own_ref[which, plane]
        for plane in range(DEPTH):
            buffer_a[which, first_on + plane, at, :] = on_ref[which, plane]
            buffer_a[which, first_off + plane, at, :] = off_ref[which, plane]


def clear_edges(buffers, rows):
    planes, lanes = buffers[0].shape[1], buffers[0].shape[3]
    blank = jnp.zeros((PAD + 16, lanes), jnp.float32)

    @pl.when(pl.program_id(0) == 0)
    def _():
        def clear(plane, _):
            for ref in buffers:
                for lead in range(2):
                    ref[lead, plane, pl.ds(0, PAD + 16), :] = blank
                    ref[lead, plane, pl.ds(rows + PAD - 16, PAD + 16), :] = blank
            return 0

        lax.fori_loop(0, planes, clear, 0)


def middle_kernel(
    first,
    window,
    next_window,
    parity_ref,
    coef_ref,
    own_in,
    on_in,
    off_in,
    w0_ref,
    inv_ref,
    own_ref,
    on_ref,
    off_ref,
    buffer_a,
    buffer_b,
):
    block = own_in.shape[1]
    rows = coef_ref.shape[2] - 2 * PAD
    parity = parity_ref[0]
    clear_edges((buffer_a, buffer_b), rows)
    load_in(parity, own_in, on_in, off_in, buffer_a, block, window)
    chunks = range(1, rows // 8 - 1)
    result = sweeps_on((buffer_a, buffer_b), coef_ref, w0_ref, inv_ref, first, block, chunks, 2, 8)
    send_out(result, parity, own_ref, on_ref, off_ref, block, next_window)


def last_kernel(
    first,
    window,
    parity_ref,
    table_ref,
    coef_ref,
    own_in,
    on_in,
    off_in,
    w0_ref,
    inv_ref,
    out_ref,
    buffer_a,
    buffer_b,
):
    pair = pl.program_id(0)
    block = own_in.shape[1]
    total, chunk_rows = out_ref.shape[0], out_ref.shape[2]
    rows = coef_ref.shape[2] - 2 * PAD
    clear_edges((buffer_a, buffer_b), rows)
    load_in(parity_ref[0], own_in, on_in, off_in, buffer_a, block, window)
    chunks = range(1, rows // 8 - 1)
    result = sweeps_on((buffer_a, buffer_b), coef_ref, w0_ref, inv_ref, first, block, chunks, 2, 8)
    own = DEPTH + 1

    def gather(keep):
        def one(plane, _):
            for chunk in range(chunk_rows // 8):
                at = pl.ds(8 * chunk, 8)
                row = pl.ds(PAD + YHALO + 8 * chunk, 8)
                w_a = result[0, own + plane, row, :]
                w_b = result[1, own + plane, row, :]
                for lead in range(total):
                    value = table_ref[lead, 2 * pair] * w_a + table_ref[lead, 2 * pair + 1] * w_b
                    if keep:
                        value = value + out_ref[lead, plane, at, :]
                    out_ref[lead, plane, at, :] = value
            return 0

        lax.fori_loop(0, block, one, 0)

    @pl.when(pair == 0)
    def _():
        gather(False)

    @pl.when(pair > 0)
    def _():
        gather(True)


def shards(state, start_field, diffusivity, time_weights, shift_real, shift_imag):
    steps, block, length, lanes = state.shape
    pieces = lax.axis_size("tm")
    slabs = lax.axis_size("gx")
    total = steps * pieces
    pairs = total // 2
    chunk = length // pieces
    rows = chunk + 2 * YHALO
    own = DEPTH + 1
    planes = block + 2 * own
    padded = rows + 2 * PAD
    f32 = jnp.float32
    device = lax.axis_index("tm")
    parity = (lax.axis_index("gx") % 2).astype(jnp.int32).reshape((1,))
    on_pairs = [(i, i ^ 1) for i in range(slabs)]
    off_pairs = []
    for i in range(1, slabs - 1, 2):
        off_pairs += [(i, i + 1), (i + 1, i)]

    def swap_on(value):
        return lax.ppermute(value, "gx", on_pairs)

    def swap_off(value):
        return lax.ppermute(value, "gx", off_pairs)

    plane_spec = pl.BlockSpec((1, 1, length, lanes), lambda i, j: (i, j, 0, 0))
    packed = pl.pallas_call(
        functools.partial(pack_kernel, chunk),
        grid=(steps, block),
        in_specs=[SMEM, plane_spec],
        out_specs=pl.BlockSpec((pieces, 1, 1, rows, lanes), lambda i, j: (0, i, j, 0, 0)),
        out_shape=jax.ShapeDtypeStruct((pieces, steps, block, rows, lanes), f32),
        name="pack",
    )(time_weights, state)
    mixed = lax.all_to_all(packed, "tm", split_axis=0, concat_axis=0, tiled=True)
    mixed = mixed.reshape((total, block, rows, lanes))

    fixed = jnp.pad(jnp.stack([start_field, diffusivity]), ((0, 0), (0, 0), (YHALO, YHALO), (0, 0)))
    fixed = lax.dynamic_slice_in_dim(fixed, device * chunk, rows, axis=2)
    fixed_off = swap_off(fixed)
    fixed_on = swap_on(fixed)
    mixed_off = swap_off(mixed)
    mixed_on = swap_on(mixed)

    def window_of(done):
        halo = SWEEPS - done
        low = (YHALO - halo) // 4 * 4
        return low, rows - 2 * low

    windows = [window_of(DEPTH * (i + 1)) for i in range(SWEEPS // DEPTH - 1)]

    def pair_spec(count, *rest):
        return pl.BlockSpec((count,) + rest, lambda i: (i,) + (0,) * len(rest))

    def traffic(window):
        low, size = window
        specs = [pair_spec(2, block, size, lanes)] + [pair_spec(2, DEPTH, size, lanes)] * 2
        shapes = [jax.ShapeDtypeStruct((total, block, size, lanes), f32)]
        shapes += [jax.ShapeDtypeStruct((total, DEPTH, size, lanes), f32)] * 2
        return specs, shapes

    kept_specs = [pair_spec(2, planes - 4, rows - 16, lanes), pair_spec(3, planes - 4, rows - 16, lanes)]
    kept_shapes = [
        jax.ShapeDtypeStruct((total, planes - 4, rows - 16, lanes), f32),
        jax.ShapeDtypeStruct((3 * pairs, planes - 4, rows - 16, lanes), f32),
    ]
    buffers = [pltpu.VMEM((2, planes, padded, lanes), f32)] * 2
    params = pltpu.CompilerParams(vmem_limit_bytes=48 * 1024 * 1024)

    specs, shapes = traffic(windows[0])
    own_w, on_w, off_w, w0, inverse, coefs = pl.pallas_call(
        functools.partial(setup_kernel, windows[0]),
        grid=(pairs,),
        in_specs=[SMEM] * 4 + [VMEM] * 6,
        out_specs=specs + kept_specs + [VMEM],
        out_shape=shapes + kept_shapes + [jax.ShapeDtypeStruct((3, planes, padded, lanes), f32)],
        scratch_shapes=[
            pltpu.VMEM((total, planes, padded, lanes), f32),
            pltpu.VMEM((2, planes, padded, lanes), f32),
            pltpu.VMEM((planes, rows, lanes), f32),
            pltpu.VMEM((total, planes, rows, lanes), f32),
            pltpu.VMEM((2, planes, rows, lanes), f32),
            pltpu.VMEM((3, planes, rows, lanes), f32),
        ]
        + buffers,
        compiler_params=params,
        name="setup",
    )(
        parity,
        jnp.asarray(forward_table(total), f32),
        shift_real,
        shift_imag,
        mixed,
        mixed_on,
        mixed_off,
        fixed,
        fixed_on,
        fixed_off,
    )
    for phase in range(1, SWEEPS // DEPTH):
        window = windows[phase - 1]
        off_in = swap_off(off_w)
        on_in = swap_on(on_w)
        in_specs = traffic(window)[0]
        if phase < SWEEPS // DEPTH - 1:
            specs, shapes = traffic(windows[phase])
            own_w, on_w, off_w = pl.pallas_call(
                functools.partial(middle_kernel, DEPTH * phase, window, windows[phase]),
                grid=(pairs,),
                in_specs=[SMEM, VMEM] + in_specs + kept_specs,
                out_specs=specs,
                out_shape=shapes,
                scratch_shapes=buffers,
                compiler_params=params,
                name=f"middle{phase}",
            )(parity, coefs, own_w, on_in, off_in, w0, inverse)
        else:
            delta = pl.pallas_call(
                functools.partial(last_kernel, DEPTH * phase, window),
                grid=(pairs,),
                in_specs=[SMEM, SMEM, VMEM] + in_specs + kept_specs,
                out_specs=VMEM,
                out_shape=jax.ShapeDtypeStruct((total, block, chunk, lanes), f32),
                scratch_shapes=buffers,
                compiler_params=params,
                name="last",
            )(
                parity,
                jnp.asarray(inverse_table(total), f32),
                coefs,
                own_w,
                on_in,
                off_in,
                w0,
                inverse,
            )
    back = lax.all_to_all(
        delta.reshape((pieces, steps, block, chunk, lanes)), "tm", split_axis=0, concat_axis=0, tiled=True
    )
    return pl.pallas_call(
        functools.partial(finish_kernel, total),
        grid=(steps, block),
        in_specs=[
            SMEM,
            plane_spec,
            pl.BlockSpec((pieces, 1, 1, chunk, lanes), lambda i, j: (0, i, j, 0, 0)),
        ],
        out_specs=plane_spec,
        out_shape=jax.ShapeDtypeStruct((steps, block, length, lanes), f32),
        name="finish",
    )(time_weights, state, back)


def solution(mesh):
    in_specs = (
        P("tm", "gx", None, None),
        P("gx", None, None),
        P("gx", None, None),
        P("tm"),
        P(),
        P(),
    )
    out_specs = P("tm", "gx", None, None)
    return jax.shard_map(shards, mesh=mesh, in_specs=in_specs, out_specs=out_specs, check_vma=False)
```

```python
import functools
import math

import jax
import jax.numpy as jnp
import numpy as np
from jax import lax
from jax.experimental import pallas as pl
from jax.experimental.pallas import tpu as pltpu
from jax.sharding import PartitionSpec as P

SWEEPS = 12
DEPTH = 3
YHALO = 16
PAD = 8
GROUPS = 2
LIMIT = 24 * 1024 * 1024
COST = 5_000_000

cheb_centre = 1.0
cheb_half = 0.7

VMEM = pl.BlockSpec(memory_space=pltpu.VMEM)
SMEM = pl.BlockSpec(memory_space=pltpu.SMEM)


def omegas():
    return [
        1.0
        / (cheb_centre + cheb_half * math.cos(math.pi * (2 * turn + 1) / (2 * SWEEPS)))
        for turn in range(SWEEPS)
    ]


def mode_terms(total):
    time = np.arange(total)
    table = np.zeros((total, total))
    table[0] = 1.0
    table[1] = np.where(time % 2 == 0, 1.0, -1.0)
    for mode in range(1, total // 2):
        angle = 2.0 * np.pi * (mode * time % total) / total
        table[2 * mode] = np.cos(angle)
        table[2 * mode + 1] = -np.sin(angle)
    table[np.abs(table) < 1e-9] = 0.0
    return table


def weighted(values, weights):
    groups = {}
    for value, weight in zip(values, weights):
        size = round(abs(float(weight)), 12)
        if size == 0.0:
            continue
        sign = 1 if weight > 0 else -1
        groups.setdefault(size, []).append((sign, value))
    total = None
    for size, members in groups.items():
        sign, part = members[0]
        lead = sign
        for sign, value in members[1:]:
            part = part + value if sign == lead else part - value
        factor = lead * size
        if factor != 1.0:
            part = part * factor
        total = part if total is None else total + part
    return total


def spectra(values):
    total = len(values)
    half = total // 2
    table = mode_terms(total)
    even = [values[0]] + [values[n] + values[total - n] for n in range(1, half)] + [values[half]]
    odd = [values[n] - values[total - n] for n in range(1, half)]
    fields = [weighted(even, table[0][: half + 1]), weighted(even, table[1][: half + 1])]
    for mode in range(1, half):
        fields.append(weighted(even, table[2 * mode][: half + 1]))
        fields.append(weighted(odd, table[2 * mode + 1][1:half]))
    return fields


def near_sum(w_ref, lead, coef_ref, plane, row, shift=0):
    lanes = w_ref.shape[-1]
    at = pl.ds(row, 8)
    below = pl.ds(row - 1, 8)
    above = pl.ds(row + 1, 8)
    mine = plane - shift
    core = w_ref[lead, mine, at, :]
    face = coef_ref[2, plane, at, :]
    total = coef_ref[0, plane, at, :] * w_ref[lead, mine - 1, at, :]
    total = total + coef_ref[0, plane + 1, at, :] * w_ref[lead, mine + 1, at, :]
    total = total + coef_ref[1, plane, at, :] * w_ref[lead, mine, below, :]
    total = total + coef_ref[1, plane, above, :] * w_ref[lead, mine, above, :]
    total = total + face * pltpu.roll(core, 1, 1)
    total = total + pltpu.roll(face * core, lanes - 1, 1)
    return core, total


def sweep(source, target, coef_ref, w0_ref, inv_ref, pair, omega, planes, chunks):
    first, count = planes

    def two(turn, _):
        for side in range(2):
            plane = first + 2 * turn + side
            for chunk in chunks:
                row = PAD + 8 * chunk
                at = pl.ds(8 * chunk, 8)
                core_a, sum_a = near_sum(source, 0, coef_ref, plane, row)
                core_b, sum_b = near_sum(source, 1, coef_ref, plane, row)
                inv_a = inv_ref[3 * pair, plane - 1, at, :]
                inv_b = inv_ref[3 * pair + 1, plane - 1, at, :]
                cross = inv_ref[3 * pair + 2, plane - 1, at, :]
                term_a = w0_ref[2 * pair, plane - 1, at, :] + (inv_a * sum_a - cross * sum_b)
                term_b = w0_ref[2 * pair + 1, plane - 1, at, :] + (inv_b * sum_b + cross * sum_a)
                target[0, plane, pl.ds(row, 8), :] = (1.0 - omega) * core_a + omega * term_a
                target[1, plane, pl.ds(row, 8), :] = (1.0 - omega) * core_b + omega * term_b
        return 0

    lax.fori_loop(0, count // 2, two, 0)


def chunks_of(rows, halo):
    first = (YHALO - halo) // 8
    return range(max(first, 0), min(rows // 8 - first, rows // 8))


def sweeps_on(buffers, coef_ref, w0_ref, inv_ref, pair, done, block, rows):
    own = DEPTH + 1
    for step in range(DEPTH):
        reach = DEPTH - 1 - step
        sweep(
            buffers[step % 2],
            buffers[(step + 1) % 2],
            coef_ref,
            w0_ref,
            inv_ref,
            pair,
            omegas()[done + step],
            (own - reach, block + 2 * reach),
            chunks_of(rows, SWEEPS - 1 - done - step),
        )
    return buffers[DEPTH % 2]


def send_out(result, pair, parity, own_ref, on_ref, off_ref, block, own_window, window):
    own = DEPTH + 1
    first_on = own + jnp.where(parity == 0, block - DEPTH, 0)
    first_off = own + jnp.where(parity == 0, 0, block - DEPTH)
    own_at = pl.ds(PAD + own_window[0], own_window[1])
    at = pl.ds(PAD + window[0], window[1])
    for which in range(2):
        for plane in range(DEPTH):
            off_ref[2 * pair + which, plane] = result[which, first_off + plane, at, :]
            on_ref[2 * pair + which, plane] = result[which, first_on + plane, at, :]
        for plane in range(block):
            own_ref[2 * pair + which, plane] = result[which, own + plane, own_at, :]


def load_in(buffer_a, pair, parity, own_ref, on_ref, off_ref, block, own_window, window):
    own = DEPTH + 1
    own_at = pl.ds(PAD + own_window[0], own_window[1])
    at = pl.ds(PAD + window[0], window[1])
    first_on = jnp.where(parity == 0, own + block, 1)
    first_off = jnp.where(parity == 0, 1, own + block)
    for which in range(2):
        for plane in range(block):
            buffer_a[which, own + plane, own_at, :] = own_ref[2 * pair + which, plane]
        for plane in range(DEPTH):
            buffer_a[which, first_on + plane, at, :] = on_ref[2 * pair + which, plane]
            buffer_a[which, first_off + plane, at, :] = off_ref[2 * pair + which, plane]


def clear_edges(refs, rows, depth):
    blank = jnp.zeros((PAD + depth, refs[0].shape[-1]), jnp.float32)

    def clear(plane, _):
        for ref in refs:
            for lead in range(ref.shape[0]):
                ref[lead, plane, pl.ds(0, PAD + depth), :] = blank
                ref[lead, plane, pl.ds(rows + PAD - depth, PAD + depth), :] = blank
        return 0

    lax.fori_loop(0, refs[0].shape[1], clear, 0)


def pack_kernel(chunk, weights_ref, state_ref, out_ref):
    step = pl.program_id(0)
    pieces, _, block, rows, lanes = out_ref.shape
    length = state_ref.shape[2]
    for plane in range(block):
        for piece in range(pieces):
            low = piece * chunk - YHALO
            first, last = max(low, 0), min(low + rows, length)
            if first > low:
                out_ref[piece, 0, plane, pl.ds(0, first - low), :] = jnp.zeros(
                    (first - low, lanes), jnp.float32
                )
            if last < low + rows:
                out_ref[piece, 0, plane, pl.ds(last - low, low + rows - last), :] = jnp.zeros(
                    (low + rows - last, lanes), jnp.float32
                )
            out_ref[piece, 0, plane, pl.ds(first - low, last - first), :] = state_ref[
                0, plane, pl.ds(first, last - first), :
            ]
    for piece in range(pieces):
        out_ref[piece, 0, 0, pl.ds(0, 1), :] = jnp.full((1, lanes), weights_ref[step], jnp.float32)


def finish_kernel(weights_ref, state_ref, back_ref, out_ref):
    step = pl.program_id(0)
    pieces, _, block, chunk, lanes = back_ref.shape
    weight = jnp.full((8, lanes), weights_ref[step], jnp.float32)
    scale = (1.0 / weight)[:1]
    for plane in range(block):
        for piece in range(pieces):
            at = pl.ds(piece * chunk, chunk)
            out_ref[0, plane, at, :] = state_ref[0, plane, at, :] + back_ref[piece, 0, plane] * scale


def residual_starts(wide, base, planes, state_own, field_of, coef_ref, diag_ref, inv_ref, w0_refs):
    total = wide.shape[0]
    rows = diag_ref.shape[1]
    half = total // 2
    first, count = planes

    def one(turn, _):
        plane = first + turn
        for chunk in range(rows // 8):
            row = PAD + 8 * chunk
            at = pl.ds(8 * chunk, 8)
            around = diag_ref[plane - 1, at, :]
            values = []
            for lead in range(total):
                core, near = near_sum(wide, lead, coef_ref, plane, row, base)
                if lead == 0:
                    prior = field_of(plane, row)
                else:
                    prior = wide[lead - 1, plane - base, pl.ds(row, 8), :]
                value = prior - (around * core - near) - core * core * core
                values.append(value * state_own[lead, 0, pl.ds(0, 1), :])
            fields = spectra(values)
            for pair in range(half):
                spec_a, spec_b = fields[2 * pair], fields[2 * pair + 1]
                inv_a = inv_ref[3 * pair, plane - 1, at, :]
                inv_b = inv_ref[3 * pair + 1, plane - 1, at, :]
                cross = inv_ref[3 * pair + 2, plane - 1, at, :]
                w_a = inv_a * spec_a - cross * spec_b
                w_b = inv_b * spec_b + cross * spec_a
                put(w0_refs, 2 * pair, plane - 1, at, w_a)
                put(w0_refs, 2 * pair + 1, plane - 1, at, w_b)
        return 0

    lax.fori_loop(0, count, one, 0)


def put(refs, lead, plane, at, value):
    per = refs[0].shape[0]
    refs[lead // per][lead % per, plane, at, :] = value


def early_kernel(
    parity_ref,
    shift_real_ref,
    shift_imag_ref,
    state_own,
    state_on,
    fixed_own,
    fixed_on,
    fixed_off,
    coef_ref,
    diag_ref,
    inv_ref,
    w0_ref,
    wide,
    fixed,
):
    total, block, rows, lanes = state_own.shape
    half = total // 2
    own = DEPTH + 1
    planes = block + 2 * own
    parity = parity_ref[0]
    first_on = jnp.where(parity == 0, own + block, 0)
    first_off = jnp.where(parity == 0, 0, own + block)
    base = jnp.where(parity == 0, own, 0)
    clear_edges((fixed, coef_ref), rows, 0)
    clear_edges((wide,), rows, 0)
    body = pl.ds(PAD, rows)

    def place(plane, _):
        for lead in range(total):
            wide[lead, own - base + plane, body, :] = state_own[lead, plane]
            wide[lead, first_on - base + plane, body, :] = state_on[lead, plane]
        for lead in range(2):
            fixed[lead, own + plane, body, :] = fixed_own[lead, plane]
            fixed[lead, first_on + plane, body, :] = fixed_on[lead, plane]
            fixed[lead, first_off + plane, body, :] = fixed_off[lead, plane]
        return 0

    lax.fori_loop(0, block, place, 0)
    lane = lax.broadcasted_iota(jnp.int32, (8, lanes), 1)

    def faces(plane, _):
        for chunk in range(rows // 8):
            row = PAD + 8 * chunk
            at = pl.ds(row, 8)
            kappa = fixed[1, plane, at, :]
            coef_ref[0, plane, at, :] = 0.5 * (fixed[1, plane - 1, at, :] + kappa)
            coef_ref[1, plane, at, :] = 0.5 * (fixed[1, plane, pl.ds(row - 1, 8), :] + kappa)
            near = 0.5 * (pltpu.roll(kappa, 1, 1) + kappa)
            coef_ref[2, plane, at, :] = jnp.where(lane == 0, 0.0, near)
        return 0

    lax.fori_loop(1, planes, faces, 0)
    reals = [shift_real_ref[mode] for mode in range(half + 1)]
    imags = [shift_imag_ref[mode] for mode in range(half)]

    def inverses(plane, _):
        for chunk in range(rows // 8):
            row = PAD + 8 * chunk
            at = pl.ds(row, 8)
            out = pl.ds(8 * chunk, 8)
            kappa = fixed[1, plane, at, :]
            low = 0.5 * (kappa + jnp.where(lane == 0, 0.0, pltpu.roll(kappa, 1, 1)))
            high = 0.5 * (kappa + jnp.where(lane == lanes - 1, 0.0, pltpu.roll(kappa, lanes - 1, 1)))
            around = coef_ref[0, plane, at, :] + coef_ref[0, plane + 1, at, :]
            around = around + coef_ref[1, plane, at, :]
            around = around + coef_ref[1, plane, pl.ds(row + 1, 8), :]
            around = around + low + high
            diag_ref[plane - 1, out, :] = around
            inside = kappa > 0.0
            zero = jnp.zeros_like(kappa)
            inv_ref[0, plane - 1, out, :] = jnp.where(inside, 1.0 / (reals[0] + around), 0.0)
            inv_ref[1, plane - 1, out, :] = jnp.where(inside, 1.0 / (reals[half] + around), 0.0)
            inv_ref[2, plane - 1, out, :] = zero
            for mode in range(1, half):
                denom = reals[mode] + around
                scale = jnp.where(inside, 1.0 / (denom * denom + imags[mode] * imags[mode]), 0.0)
                value = denom * scale
                inv_ref[3 * mode, plane - 1, out, :] = value
                inv_ref[3 * mode + 1, plane - 1, out, :] = value
                inv_ref[3 * mode + 2, plane - 1, out, :] = -imags[mode] * scale
        return 0

    lax.fori_loop(1, planes - 1, inverses, 0)

    def field_of(plane, row):
        return fixed[0, plane, pl.ds(row, 8), :]

    count = block + own - 2
    first = jnp.where(parity == 0, planes - 1 - count, 1)
    residual_starts(
        wide, base, (first, count), state_own, field_of, coef_ref, diag_ref, inv_ref, (w0_ref,)
    )


def late_kernel(
    parity_ref,
    state_own,
    state_off,
    fixed_own,
    fixed_off,
    coef_ref,
    diag_ref,
    inv_ref,
    w0_in,
    *rest,
):
    w0_refs, wide, field = rest[:-2], rest[-2], rest[-1]
    total, block, rows, lanes = state_own.shape
    own = DEPTH + 1
    planes = block + 2 * own
    parity = parity_ref[0]
    base = jnp.where(parity == 0, 0, planes - own - 2)
    first_off = jnp.where(parity == 0, 0, 2)
    first_own = jnp.where(parity == 0, own, 0)
    from_own = jnp.where(parity == 0, 0, block - 2)
    clear_edges((wide,), rows, 0)
    body = pl.ds(PAD, rows)

    def place_off(plane, _):
        for lead in range(total):
            wide[lead, first_off + plane, body, :] = state_off[lead, plane]
        field[first_off + plane, body, :] = fixed_off[0, plane]
        return 0

    def place_own(plane, _):
        for lead in range(total):
            wide[lead, first_own + plane, body, :] = state_own[lead, from_own + plane]
        field[first_own + plane, body, :] = fixed_own[0, from_own + plane]
        return 0

    lax.fori_loop(0, block, place_off, 0)
    lax.fori_loop(0, 2, place_own, 0)
    count = block + own - 2
    first = jnp.where(parity == 0, planes - 1 - count, 1)

    def copy(turn, _):
        for lead in range(total):
            put(w0_refs, lead, first - 1 + turn, slice(None), w0_in[lead, first - 1 + turn])
        return 0

    lax.fori_loop(0, count, copy, 0)

    def field_of(plane, row):
        return field[plane - base, pl.ds(row, 8), :]

    residual_starts(
        wide, base, (base + 1, own), state_own, field_of, coef_ref, diag_ref, inv_ref, w0_refs
    )


def first_kernel(
    low_pair,
    own_window,
    window,
    parity_ref,
    coef_ref,
    w0_ref,
    inv_ref,
    own_ref,
    on_ref,
    off_ref,
    buffer_a,
    buffer_b,
):
    parity = parity_ref[0]
    block = own_ref.shape[1]
    rows = w0_ref.shape[2]
    clear_edges((buffer_a, buffer_b), rows, 0)
    group_inv = inv_ref.at[pl.ds(3 * low_pair, 3 * (w0_ref.shape[0] // 2))]

    def one(pair, _):
        def copy(plane, _):
            for which in range(2):
                buffer_a[which, plane + 1, pl.ds(PAD, rows), :] = w0_ref[2 * pair + which, plane]
            return 0

        lax.fori_loop(0, w0_ref.shape[1], copy, 0)
        result = sweeps_on((buffer_a, buffer_b), coef_ref, w0_ref, group_inv, pair, 0, block, rows)
        send_out(result, pair, parity, own_ref, on_ref, off_ref, block, own_window, window)
        return 0

    lax.fori_loop(0, w0_ref.shape[0] // 2, one, 0)


def middle_kernel(
    low_pair,
    done,
    windows,
    next_windows,
    parity_ref,
    coef_ref,
    own_in,
    on_in,
    off_in,
    w0_ref,
    inv_ref,
    own_ref,
    on_ref,
    off_ref,
    buffer_a,
    buffer_b,
):
    parity = parity_ref[0]
    block = own_in.shape[1]
    rows = w0_ref.shape[2]
    clear_edges((buffer_a, buffer_b), rows, 16)
    group_inv = inv_ref.at[pl.ds(3 * low_pair, 3 * (w0_ref.shape[0] // 2))]

    def one(pair, _):
        load_in(buffer_a, pair, parity, own_in, on_in, off_in, block, *windows)
        result = sweeps_on((buffer_a, buffer_b), coef_ref, w0_ref, group_inv, pair, done, block, rows)
        send_out(result, pair, parity, own_ref, on_ref, off_ref, block, *next_windows)
        return 0

    lax.fori_loop(0, w0_ref.shape[0] // 2, one, 0)


def last_kernel(low_pair, done, windows, parity_ref, coef_ref, own_in, on_in, off_in, w0_ref, inv_ref, *rest):
    out_ref, buffer_a, buffer_b = rest[-3:]
    parity = parity_ref[0]
    block = own_in.shape[1]
    rows = w0_ref.shape[2]
    total, chunk_rows = out_ref.shape[0], out_ref.shape[2]
    pairs = w0_ref.shape[0] // 2
    own = DEPTH + 1
    clear_edges((buffer_a, buffer_b), rows, 16)
    group_inv = inv_ref.at[pl.ds(3 * low_pair, 3 * pairs)]
    table = mode_terms(total).T / total
    table[:, 2:] *= 2.0
    half = total // 2
    for pair in range(pairs):
        mode = low_pair + pair
        load_in(buffer_a, pair, parity, own_in, on_in, off_in, block, *windows)
        result = sweeps_on((buffer_a, buffer_b), coef_ref, w0_ref, group_inv, pair, done, block, rows)
        before = None
        if pair > 0:
            before = out_ref
        elif len(rest) == 4:
            before = rest[0]

        def one(plane, _):
            for chunk in range(chunk_rows // 8):
                at = pl.ds(8 * chunk, 8)
                row = pl.ds(PAD + YHALO + 8 * chunk, 8)
                w_a = result[0, own + plane, row, :]
                w_b = result[1, own + plane, row, :]
                for lead in range(total):
                    value = weighted((w_a, w_b), table[lead, 2 * mode : 2 * mode + 2])
                    if before is not None:
                        value = value + before[lead, plane, at, :]
                    out_ref[lead, plane, at, :] = value
            return 0

        lax.fori_loop(0, block, one, 0)


def shards(state, start_field, diffusivity, time_weights, shift_real, shift_imag):
    steps, block, length, lanes = state.shape
    pieces = lax.axis_size("tm")
    slabs = lax.axis_size("gx")
    total = steps * pieces
    pairs = total // 2
    per = pairs // GROUPS
    chunk = length // pieces
    rows = chunk + 2 * YHALO
    own = DEPTH + 1
    planes = block + 2 * own
    padded = rows + 2 * PAD
    f32 = jnp.float32
    device = lax.axis_index("tm")
    parity = (lax.axis_index("gx") % 2).astype(jnp.int32).reshape((1,))
    on_pairs = [(i, i ^ 1) for i in range(slabs)]
    off_pairs = []
    for i in range(1, slabs - 1, 2):
        off_pairs += [(i, i + 1), (i + 1, i)]

    def shape(*dims):
        return jax.ShapeDtypeStruct(dims, f32)

    def swap_on(value, name):
        with jax.named_scope(f"{name}_on"):
            return lax.ppermute(value, "gx", on_pairs)

    def swap_off(value, name):
        with jax.named_scope(f"{name}_off"):
            return lax.ppermute(value, "gx", off_pairs)

    def call(kernel, name, inputs, scalars, outs, scratch, flops):
        return pl.pallas_call(
            kernel,
            in_specs=[SMEM] * scalars + [VMEM] * (len(inputs) - scalars),
            out_specs=[VMEM] * len(outs),
            out_shape=outs,
            scratch_shapes=[pltpu.VMEM(dims, f32) for dims in scratch],
            compiler_params=pltpu.CompilerParams(vmem_limit_bytes=LIMIT),
            cost_estimate=pl.CostEstimate(flops=flops, bytes_accessed=flops, transcendentals=0),
            name=name,
        )(*inputs)

    fixed = jnp.pad(jnp.stack([start_field, diffusivity]), ((0, 0), (0, 0), (YHALO, YHALO), (0, 0)))
    fixed = lax.dynamic_slice_in_dim(fixed, device * chunk, rows, axis=2)
    fixed_off = swap_off(fixed, "fixed")
    fixed_on = swap_on(fixed, "fixed")

    step_spec = pl.BlockSpec((1, block, length, lanes), lambda i: (i, 0, 0, 0))
    packed = pl.pallas_call(
        functools.partial(pack_kernel, chunk),
        grid=(steps,),
        in_specs=[SMEM, step_spec],
        out_specs=pl.BlockSpec((pieces, 1, block, rows, lanes), lambda i: (0, i, 0, 0, 0)),
        out_shape=shape(pieces, steps, block, rows, lanes),
        name="pack",
    )(time_weights, state)
    with jax.named_scope("mix"):
        mixed = lax.all_to_all(packed, "tm", split_axis=0, concat_axis=0, tiled=True)
    mixed = mixed.reshape((total, block, rows, lanes))
    mixed_off = swap_off(mixed, "state")
    mixed_on = swap_on(mixed, "state")

    def window_of(halo):
        low = (YHALO - halo) // 4 * 4
        return low, rows - 2 * low

    windows = []
    for phase in range(1, SWEEPS // DEPTH):
        left = SWEEPS - DEPTH * phase
        windows.append((window_of(left), window_of(left - 1)))

    coefs, diag, inverse, w0 = call(
        early_kernel,
        "early",
        (parity, shift_real, shift_imag, mixed, mixed_on, fixed, fixed_on, fixed_off),
        3,
        [
            shape(3, planes, padded, lanes),
            shape(planes - 2, rows, lanes),
            shape(3 * pairs, planes - 2, rows, lanes),
            shape(total, planes - 2, rows, lanes),
        ],
        [(total, planes - own, padded, lanes), (2, planes, padded, lanes)],
        COST,
    )
    starts = call(
        late_kernel,
        "late",
        (parity, mixed, mixed_off, fixed, fixed_off, coefs, diag, inverse, w0),
        1,
        [shape(2 * per, planes - 2, rows, lanes)] * GROUPS,
        [(total, own + 2, padded, lanes), (own + 2, padded, lanes)],
        COST,
    )
    buffers = [(2, planes, padded, lanes)] * 2

    def sent(pair_windows):
        own_window, window = pair_windows
        return [
            shape(2 * per, block, own_window[1], lanes),
            shape(2 * per, DEPTH, window[1], lanes),
            shape(2 * per, DEPTH, window[1], lanes),
        ]

    moving = []
    for group in range(GROUPS):
        own_w, on_w, off_w = call(
            functools.partial(first_kernel, per * group, *windows[0]),
            f"first{group}",
            (parity, coefs, starts[group], inverse),
            1,
            sent(windows[0]),
            buffers,
            COST,
        )
        moving.append((own_w, swap_on(on_w, f"a{group}"), swap_off(off_w, f"a{group}")))
    last = SWEEPS // DEPTH - 1
    for phase in range(1, last):
        for group in range(GROUPS):
            own_w, on_w, off_w = call(
                functools.partial(
                    middle_kernel, per * group, DEPTH * phase, windows[phase - 1], windows[phase]
                ),
                f"middle{phase}{group}",
                (parity, coefs, *moving[group], starts[group], inverse),
                1,
                sent(windows[phase]),
                buffers,
                COST,
            )
            name = "abcdefgh"[phase] + str(group)
            moving[group] = (own_w, swap_on(on_w, name), swap_off(off_w, name))
    delta = ()
    for group in range(GROUPS):
        delta = call(
            functools.partial(last_kernel, per * group, DEPTH * last, windows[last - 1]),
            f"last{group}",
            (parity, coefs, *moving[group], starts[group], inverse, *delta),
            1,
            [shape(total, block, chunk, lanes)],
            buffers,
            COST,
        )
    with jax.named_scope("back"):
        back = lax.all_to_all(
            delta[0].reshape((pieces, steps, block, chunk, lanes)),
            "tm",
            split_axis=0,
            concat_axis=0,
            tiled=True,
        )
    return pl.pallas_call(
        finish_kernel,
        grid=(steps,),
        in_specs=[
            SMEM,
            step_spec,
            pl.BlockSpec((pieces, 1, block, chunk, lanes), lambda i: (0, i, 0, 0, 0)),
        ],
        out_specs=step_spec,
        out_shape=shape(steps, block, length, lanes),
        name="finish",
    )(time_weights, state, back)


def solution(mesh):
    in_specs = (
        P("tm", "gx", None, None),
        P("gx", None, None),
        P("gx", None, None),
        P("tm"),
        P(),
        P(),
    )
    out_specs = P("tm", "gx", None, None)
    return jax.shard_map(shards, mesh=mesh, in_specs=in_specs, out_specs=out_specs, check_vma=False)
```

```python
import functools
import math

import jax
import jax.numpy as jnp
import numpy as np
from jax import lax
from jax.experimental import pallas as pl
from jax.experimental.pallas import tpu as pltpu
from jax.sharding import PartitionSpec as P


SWEEPS = 12
YHALO = 16
PAD = 8
GROUPS = 2
LIMIT = 24 * 1024 * 1024
COST = 5_000_000

cheb_centre = 1.0
cheb_half = 0.7

VMEM = pl.BlockSpec(memory_space=pltpu.VMEM)
SMEM = pl.BlockSpec(memory_space=pltpu.SMEM)


def omegas():
    return [
        1.0
        / (cheb_centre + cheb_half * math.cos(math.pi * (2 * turn + 1) / (2 * SWEEPS)))
        for turn in range(SWEEPS)
    ]


def mode_terms(total):
    time = np.arange(total)
    table = np.zeros((total, total))
    table[0] = 1.0
    table[1] = np.where(time % 2 == 0, 1.0, -1.0)
    for mode in range(1, total // 2):
        angle = 2.0 * np.pi * (mode * time % total) / total
        table[2 * mode] = np.cos(angle)
        table[2 * mode + 1] = -np.sin(angle)
    table[np.abs(table) < 1e-9] = 0.0
    return table


def weighted(values, weights):
    groups = {}
    for value, weight in zip(values, weights):
        size = round(abs(float(weight)), 12)
        if size == 0.0:
            continue
        sign = 1 if weight > 0 else -1
        groups.setdefault(size, []).append((sign, value))
    total = None
    for size, members in groups.items():
        sign, part = members[0]
        lead = sign
        for sign, value in members[1:]:
            part = part + value if sign == lead else part - value
        factor = lead * size
        if factor != 1.0:
            part = part * factor
        total = part if total is None else total + part
    return total


def spectra(values):
    total = len(values)
    half = total // 2
    table = mode_terms(total)
    even = [values[0]] + [values[n] + values[total - n] for n in range(1, half)] + [values[half]]
    odd = [values[n] - values[total - n] for n in range(1, half)]
    fields = [weighted(even, table[0][: half + 1]), weighted(even, table[1][: half + 1])]
    for mode in range(1, half):
        fields.append(weighted(even, table[2 * mode][: half + 1]))
        fields.append(weighted(odd, table[2 * mode + 1][1:half]))
    return fields


def near_sum(w_ref, lead, coef_ref, plane, row, shift=0):
    lanes = w_ref.shape[-1]
    at = pl.ds(row, 8)
    below = pl.ds(row - 1, 8)
    above = pl.ds(row + 1, 8)
    mine = plane - shift
    core = w_ref[lead, mine, at, :]
    face = coef_ref[2, plane, at, :]
    total = coef_ref[0, plane, at, :] * w_ref[lead, mine - 1, at, :]
    total = total + coef_ref[0, plane + 1, at, :] * w_ref[lead, mine + 1, at, :]
    total = total + coef_ref[1, plane, at, :] * w_ref[lead, mine, below, :]
    total = total + coef_ref[1, plane, above, :] * w_ref[lead, mine, above, :]
    total = total + face * pltpu.roll(core, 1, 1)
    total = total + pltpu.roll(face * core, lanes - 1, 1)
    return core, total


def sweep(source, target, coef_ref, w0_ref, inv_ref, pair, omega, planes, chunks):
    first, count = planes

    def two(turn, _):
        for side in range(2):
            plane = first + 2 * turn + side
            for chunk in chunks:
                row = PAD + 8 * chunk
                at = pl.ds(8 * chunk, 8)
                core_a, sum_a = near_sum(source, 0, coef_ref, plane, row)
                core_b, sum_b = near_sum(source, 1, coef_ref, plane, row)
                inv_a = inv_ref[3 * pair, plane - 1, at, :]
                inv_b = inv_ref[3 * pair + 1, plane - 1, at, :]
                cross = inv_ref[3 * pair + 2, plane - 1, at, :]
                term_a = w0_ref[2 * pair, plane - 1, at, :] + (inv_a * sum_a - cross * sum_b)
                term_b = w0_ref[2 * pair + 1, plane - 1, at, :] + (inv_b * sum_b + cross * sum_a)
                target[0, plane, pl.ds(row, 8), :] = (1.0 - omega) * core_a + omega * term_a
                target[1, plane, pl.ds(row, 8), :] = (1.0 - omega) * core_b + omega * term_b
        return 0

    lax.fori_loop(0, count // 2, two, 0)


def chunks_of(rows, halo):
    first = (YHALO - halo) // 8
    return range(max(first, 0), min(rows // 8 - first, rows // 8))


def sweeps_on(buffers, coef_ref, w0_ref, inv_ref, pair, done, block, rows):
    for step in range(block):
        reach = block - 1 - step
        sweep(
            buffers[step % 2],
            buffers[(step + 1) % 2],
            coef_ref,
            w0_ref,
            inv_ref,
            pair,
            omegas()[done + step],
            (block - reach, block + 2 * reach),
            chunks_of(rows, SWEEPS - 1 - done - step),
        )
    return buffers[block % 2]


def load_in(buffer_a, pair, parity, own_ref, on_ref, off_ref, window):
    block = own_ref.shape[1]
    at = pl.ds(PAD + window[0], window[1])
    first_on = jnp.where(parity == 0, 2 * block, 0)
    first_off = jnp.where(parity == 0, 0, 2 * block)
    for which in range(2):
        for plane in range(block):
            buffer_a[which, block + plane, at, :] = own_ref[2 * pair + which, plane]
            buffer_a[which, first_on + plane, at, :] = on_ref[2 * pair + which, plane]
            buffer_a[which, first_off + plane, at, :] = off_ref[2 * pair + which, plane]


def clear_edges(refs, rows, depth):
    blank = jnp.zeros((PAD + depth, refs[0].shape[-1]), jnp.float32)

    def clear(plane, _):
        for ref in refs:
            for lead in range(ref.shape[0]):
                ref[lead, plane, pl.ds(0, PAD + depth), :] = blank
                ref[lead, plane, pl.ds(rows + PAD - depth, PAD + depth), :] = blank
        return 0

    lax.fori_loop(0, refs[0].shape[1], clear, 0)


def pack_kernel(chunk, weights_ref, state_ref, out_ref):
    step = pl.program_id(0)
    pieces, _, block, rows, lanes = out_ref.shape
    length = state_ref.shape[2]
    for plane in range(block):
        for piece in range(pieces):
            low = piece * chunk - YHALO
            first, last = max(low, 0), min(low + rows, length)
            if first > low:
                out_ref[piece, 0, plane, pl.ds(0, first - low), :] = jnp.zeros(
                    (first - low, lanes), jnp.float32
                )
            if last < low + rows:
                out_ref[piece, 0, plane, pl.ds(last - low, low + rows - last), :] = jnp.zeros(
                    (low + rows - last, lanes), jnp.float32
                )
            out_ref[piece, 0, plane, pl.ds(first - low, last - first), :] = state_ref[
                0, plane, pl.ds(first, last - first), :
            ]
    for piece in range(pieces):
        out_ref[piece, 0, 0, pl.ds(0, 1), :] = jnp.full((1, lanes), weights_ref[step], jnp.float32)


def finish_kernel(weights_ref, state_ref, back_ref, out_ref):
    step = pl.program_id(0)
    pieces, _, block, chunk, lanes = back_ref.shape
    weight = jnp.full((8, lanes), weights_ref[step], jnp.float32)
    scale = (1.0 / weight)[:1]
    for plane in range(block):
        for piece in range(pieces):
            at = pl.ds(piece * chunk, chunk)
            out_ref[0, plane, at, :] = state_ref[0, plane, at, :] + back_ref[piece, 0, plane] * scale


def residual_starts(wide, base, planes, state_own, field_of, coef_ref, diag_ref, inv_ref, w0_ref, w0_base):
    total = wide.shape[0]
    rows = diag_ref.shape[1]
    half = total // 2
    first, count = planes

    def one(turn, _):
        plane = first + turn
        for chunk in range(rows // 8):
            row = PAD + 8 * chunk
            at = pl.ds(8 * chunk, 8)
            around = diag_ref[plane - 1, at, :]
            values = []
            for lead in range(total):
                core, near = near_sum(wide, lead, coef_ref, plane, row, base)
                if lead == 0:
                    prior = field_of(plane, row)
                else:
                    prior = wide[lead - 1, plane - base, pl.ds(row, 8), :]
                value = prior - (around * core - near) - core * core * core
                values.append(value * state_own[lead, 0, pl.ds(0, 1), :])
            fields = spectra(values)
            for pair in range(half):
                spec_a, spec_b = fields[2 * pair], fields[2 * pair + 1]
                inv_a = inv_ref[3 * pair, plane - 1, at, :]
                inv_b = inv_ref[3 * pair + 1, plane - 1, at, :]
                cross = inv_ref[3 * pair + 2, plane - 1, at, :]
                w_a = inv_a * spec_a - cross * spec_b
                w_b = inv_b * spec_b + cross * spec_a
                w0_ref[2 * pair, plane - w0_base, at, :] = w_a
                w0_ref[2 * pair + 1, plane - w0_base, at, :] = w_b
        return 0

    lax.fori_loop(0, count, one, 0)


def edges_kernel(parity_ref, state_ref, on_ref, off_ref):
    block = state_ref.shape[1]
    near_on = jnp.where(parity_ref[0] == 0, block - 1, 0)

    def one(lead, _):
        on_ref[lead, 0] = state_ref[lead, near_on]
        off_ref[lead, 0] = state_ref[lead, block - 1 - near_on]
        return 0

    lax.fori_loop(0, state_ref.shape[0], one, 0)


def early_kernel(
    parity_ref,
    shift_real_ref,
    shift_imag_ref,
    state_own,
    state_on,
    fixed_own,
    fixed_on,
    fixed_off,
    coef_ref,
    diag_ref,
    inv_ref,
    w0_ref,
    wide,
    fixed,
):
    total, block, rows, lanes = state_own.shape
    half = total // 2
    planes = 3 * block
    parity = parity_ref[0]
    first_on = jnp.where(parity == 0, 2 * block, 0)
    first_off = jnp.where(parity == 0, 0, 2 * block)
    base = jnp.where(parity == 0, block, block - 1)
    clear_edges((fixed, coef_ref), rows, 0)
    clear_edges((wide,), rows, 0)
    body = pl.ds(PAD, rows)
    for lead in range(total):
        wide[lead, jnp.where(parity == 0, block, 0), body, :] = state_on[lead, 0]

    def place(plane, _):
        for lead in range(total):
            wide[lead, block - base + plane, body, :] = state_own[lead, plane]
        for lead in range(2):
            fixed[lead, block + plane, body, :] = fixed_own[lead, plane]
            fixed[lead, first_on + plane, body, :] = fixed_on[lead, plane]
            fixed[lead, first_off + plane, body, :] = fixed_off[lead, plane]
        return 0

    lax.fori_loop(0, block, place, 0)
    lane = lax.broadcasted_iota(jnp.int32, (8, lanes), 1)

    def faces(plane, _):
        for chunk in range(rows // 8):
            row = PAD + 8 * chunk
            at = pl.ds(row, 8)
            kappa = fixed[1, plane, at, :]
            coef_ref[0, plane, at, :] = 0.5 * (fixed[1, plane - 1, at, :] + kappa)
            coef_ref[1, plane, at, :] = 0.5 * (fixed[1, plane, pl.ds(row - 1, 8), :] + kappa)
            near = 0.5 * (pltpu.roll(kappa, 1, 1) + kappa)
            coef_ref[2, plane, at, :] = jnp.where(lane == 0, 0.0, near)
        return 0

    lax.fori_loop(1, planes, faces, 0)
    reals = [shift_real_ref[mode] for mode in range(half + 1)]
    imags = [shift_imag_ref[mode] for mode in range(half)]

    def inverses(plane, _):
        for chunk in range(rows // 8):
            row = PAD + 8 * chunk
            at = pl.ds(row, 8)
            out = pl.ds(8 * chunk, 8)
            kappa = fixed[1, plane, at, :]
            low = 0.5 * (kappa + jnp.where(lane == 0, 0.0, pltpu.roll(kappa, 1, 1)))
            high = 0.5 * (kappa + jnp.where(lane == lanes - 1, 0.0, pltpu.roll(kappa, lanes - 1, 1)))
            around = coef_ref[0, plane, at, :] + coef_ref[0, plane + 1, at, :]
            around = around + coef_ref[1, plane, at, :]
            around = around + coef_ref[1, plane, pl.ds(row + 1, 8), :]
            around = around + low + high
            diag_ref[plane - 1, out, :] = around
            inside = kappa > 0.0
            zero = jnp.zeros_like(kappa)
            inv_ref[0, plane - 1, out, :] = jnp.where(inside, 1.0 / (reals[0] + around), 0.0)
            inv_ref[1, plane - 1, out, :] = jnp.where(inside, 1.0 / (reals[half] + around), 0.0)
            inv_ref[2, plane - 1, out, :] = zero
            for mode in range(1, half):
                denom = reals[mode] + around
                scale = jnp.where(inside, 1.0 / (denom * denom + imags[mode] * imags[mode]), 0.0)
                value = denom * scale
                inv_ref[3 * mode, plane - 1, out, :] = value
                inv_ref[3 * mode + 1, plane - 1, out, :] = value
                inv_ref[3 * mode + 2, plane - 1, out, :] = -imags[mode] * scale
        return 0

    lax.fori_loop(1, planes - 1, inverses, 0)

    def field_of(plane, row):
        return fixed[0, plane, pl.ds(row, 8), :]

    first = jnp.where(parity == 0, block + 1, block)
    residual_starts(
        wide, base, (first, block - 1), state_own, field_of, coef_ref, diag_ref, inv_ref, w0_ref, block
    )


def late_kernel(
    window, parity_ref, state_own, state_off, fixed_own, coef_ref, diag_ref, inv_ref, w0_in, *rest
):
    w0_refs, wide, outer = rest[:-2], rest[-2], rest[-1]
    total, block, rows, _ = state_own.shape
    parity = parity_ref[0]
    base = jnp.where(parity == 0, block - 1, 2 * block - 2)
    at_off = jnp.where(parity == 0, 0, 2)
    at_own = jnp.where(parity == 0, 1, 0)
    from_own = jnp.where(parity == 0, 0, block - 2)
    clear_edges((wide,), rows, 0)
    body = pl.ds(PAD, rows)
    for lead in range(total):
        wide[lead, at_off, body, :] = state_off[lead, 0]
        wide[lead, at_own, body, :] = state_own[lead, from_own]
        wide[lead, at_own + 1, body, :] = state_own[lead, from_own + 1]

    def field_of(plane, row):
        return fixed_own[0, plane - block, pl.ds(row - PAD, 8), :]

    residual_starts(
        wide,
        base,
        (base + 1, 1),
        state_own,
        field_of,
        coef_ref,
        diag_ref,
        inv_ref,
        outer,
        base + 1,
    )
    inner = jnp.where(parity == 0, 1, 0)
    outermost = jnp.where(parity == 0, 0, block - 1)
    per = w0_refs[0].shape[0]
    at = pl.ds(*window)
    for group in range(len(w0_refs)):
        for lead in range(per):
            source = group * per + lead
            for plane in range(block - 1):
                w0_refs[group][lead, inner + plane] = w0_in[source, inner + plane, at, :]
            w0_refs[group][lead, outermost] = outer[source, 0, at, :]


def phase_kernel(
    low_pair, done, window, next_window, parity_ref, coef_ref, inv_ref, own_in, on_in, off_in, *rest
):
    buffer_a, buffer_b = rest[-2:]
    if done == 0:
        w0_ref, out_ref = rest[:2]
    else:
        w0_ref, out_ref = rest[0], rest[1]
    parity = parity_ref[0]
    pairs, block, rows = w0_ref.shape[0] // 2, own_in.shape[1], w0_ref.shape[2]
    clear_edges((buffer_a, buffer_b), rows, window[0])
    group_inv = inv_ref.at[pl.ds(3 * low_pair, 3 * pairs)]

    def one(pair, _):
        load_in(buffer_a, pair, parity, own_in, on_in, off_in, window)
        if done == 0:

            def keep(plane, _):
                for which in range(2):
                    w0_ref[2 * pair + which, plane] = buffer_a[which, plane + 1, pl.ds(PAD, rows), :]
                return 0

            lax.fori_loop(0, w0_ref.shape[1], keep, 0)
        result = sweeps_on((buffer_a, buffer_b), coef_ref, w0_ref, group_inv, pair, done, block, rows)
        at = pl.ds(PAD + next_window[0], next_window[1])
        for which in range(2):
            for plane in range(block):
                out_ref[2 * pair + which, plane] = result[which, block + plane, at, :]
        return 0

    lax.fori_loop(0, pairs, one, 0)


def last_kernel(low_pair, done, window, parity_ref, coef_ref, inv_ref, own_in, on_in, off_in, w0_ref, *rest):
    out_ref, buffer_a, buffer_b = rest[-3:]
    parity = parity_ref[0]
    pairs, block, rows = w0_ref.shape[0] // 2, own_in.shape[1], w0_ref.shape[2]
    total, chunk_rows = out_ref.shape[0], out_ref.shape[2]
    clear_edges((buffer_a, buffer_b), rows, window[0])
    group_inv = inv_ref.at[pl.ds(3 * low_pair, 3 * pairs)]
    table = mode_terms(total).T / total
    table[:, 2:] *= 2.0
    for pair in range(pairs):
        mode = low_pair + pair
        load_in(buffer_a, pair, parity, own_in, on_in, off_in, window)
        result = sweeps_on((buffer_a, buffer_b), coef_ref, w0_ref, group_inv, pair, done, block, rows)
        before = None
        if pair > 0:
            before = out_ref
        elif len(rest) == 4:
            before = rest[0]

        def one(plane, _):
            for chunk in range(chunk_rows // 8):
                at = pl.ds(8 * chunk, 8)
                row = pl.ds(PAD + YHALO + 8 * chunk, 8)
                w_a = result[0, block + plane, row, :]
                w_b = result[1, block + plane, row, :]
                for lead in range(total):
                    value = weighted((w_a, w_b), table[lead, 2 * mode : 2 * mode + 2])
                    if before is not None:
                        value = value + before[lead, plane, at, :]
                    out_ref[lead, plane, at, :] = value
            return 0

        lax.fori_loop(0, block, one, 0)


def shards(state, start_field, diffusivity, time_weights, shift_real, shift_imag):
    steps, block, length, lanes = state.shape
    pieces = lax.axis_size("tm")
    slabs = lax.axis_size("gx")
    total = steps * pieces
    pairs = total // 2
    per = pairs // GROUPS
    chunk = length // pieces
    rows = chunk + 2 * YHALO
    planes = 3 * block
    padded = rows + 2 * PAD
    f32 = jnp.float32
    device = lax.axis_index("tm")
    parity = (lax.axis_index("gx") % 2).astype(jnp.int32).reshape((1,))
    on_pairs = [(i, i ^ 1) for i in range(slabs)]
    off_pairs = []
    for i in range(1, slabs - 1, 2):
        off_pairs += [(i, i + 1), (i + 1, i)]

    def shape(*dims):
        return jax.ShapeDtypeStruct(dims, f32)

    def swap_on(value):
        return lax.ppermute(value, "gx", on_pairs)

    def swap_off(value):
        return lax.ppermute(value, "gx", off_pairs)

    def call(kernel, inputs, scalars, outs, scratch, flops):
        return pl.pallas_call(
            kernel,
            in_specs=[SMEM] * scalars + [VMEM] * (len(inputs) - scalars),
            out_specs=[VMEM] * len(outs),
            out_shape=outs,
            scratch_shapes=[pltpu.VMEM(dims, f32) for dims in scratch],
            compiler_params=pltpu.CompilerParams(vmem_limit_bytes=LIMIT),
            cost_estimate=pl.CostEstimate(flops=flops, bytes_accessed=flops, transcendentals=0),
        )(*inputs)

    fixed = jnp.pad(jnp.stack([start_field, diffusivity]), ((0, 0), (0, 0), (YHALO, YHALO), (0, 0)))
    fixed = lax.dynamic_slice_in_dim(fixed, device * chunk, rows, axis=2)
    fixed_off = swap_off(fixed)
    fixed_on = swap_on(fixed)

    step_spec = pl.BlockSpec((1, block, length, lanes), lambda i: (i, 0, 0, 0))
    packed = pl.pallas_call(
        functools.partial(pack_kernel, chunk),
        grid=(steps,),
        in_specs=[SMEM, step_spec],
        out_specs=pl.BlockSpec((pieces, 1, block, rows, lanes), lambda i: (0, i, 0, 0, 0)),
        out_shape=shape(pieces, steps, block, rows, lanes),
        name="pack",
    )(time_weights, state)
    mixed = lax.all_to_all(packed, "tm", split_axis=0, concat_axis=0, tiled=True)
    mixed = mixed.reshape((total, block, rows, lanes))
    edge = shape(total, 1, rows, lanes)
    edge_on, edge_off = call(edges_kernel, (parity, mixed), 1, [edge] * 2, [], COST // 10)
    mixed_off = swap_off(edge_off)
    mixed_on = swap_on(edge_on)

    windows = []
    for left in range(SWEEPS, 0, -block):
        low = (YHALO - left) // 4 * 4
        windows.append((low, rows - 2 * low))

    coefs, diag, inverse, w0 = call(
        early_kernel,
        (parity, shift_real, shift_imag, mixed, mixed_on, fixed, fixed_on, fixed_off),
        3,
        [
            shape(3, planes, padded, lanes),
            shape(planes - 2, rows, lanes),
            shape(3 * pairs, planes - 2, rows, lanes),
            shape(total, block, rows, lanes),
        ],
        [(total, block + 1, padded, lanes), (2, planes, padded, lanes)],
        COST,
    )
    values = call(
        functools.partial(late_kernel, windows[0]),
        (parity, mixed, mixed_off, fixed, coefs, diag, inverse, w0),
        1,
        [shape(2 * per, block, windows[0][1], lanes)] * GROUPS,
        [(total, 3, padded, lanes), (total, 1, rows, lanes)],
        COST // 4,
    )
    buffers = [(2, planes, padded, lanes)] * 2

    def exchange(value):
        return value, swap_on(value), swap_off(value)

    moving = [exchange(values[group]) for group in range(GROUPS)]
    starts = [None] * GROUPS
    last = len(windows) - 1
    for phase in range(last):
        for group in range(GROUPS):
            outs = [shape(2 * per, block, windows[phase + 1][1], lanes)]
            extra = ()
            if phase == 0:
                outs = [shape(2 * per, planes - 2, rows, lanes)] + outs
            else:
                extra = (starts[group],)
            results = call(
                functools.partial(
                    phase_kernel, per * group, block * phase, windows[phase], windows[phase + 1]
                ),
                (parity, coefs, inverse, *moving[group], *extra),
                1,
                outs,
                buffers,
                COST,
            )
            if phase == 0:
                starts[group] = results[0]
            moving[group] = exchange(results[-1])
    delta = ()
    for group in range(GROUPS):
        delta = call(
            functools.partial(last_kernel, per * group, block * last, windows[last]),
            (parity, coefs, inverse, *moving[group], starts[group], *delta),
            1,
            [shape(total, block, chunk, lanes)],
            buffers,
            COST,
        )
    back = lax.all_to_all(
        delta[0].reshape((pieces, steps, block, chunk, lanes)),
        "tm",
        split_axis=0,
        concat_axis=0,
        tiled=True,
    )
    return pl.pallas_call(
        finish_kernel,
        grid=(steps,),
        in_specs=[
            SMEM,
            step_spec,
            pl.BlockSpec((pieces, 1, block, chunk, lanes), lambda i: (0, i, 0, 0, 0)),
        ],
        out_specs=step_spec,
        out_shape=shape(steps, block, length, lanes),
        name="finish",
    )(time_weights, state, back)


def solution(mesh):
    in_specs = (
        P("tm", "gx", None, None),
        P("gx", None, None),
        P("gx", None, None),
        P("tm"),
        P(),
        P(),
    )
    out_specs = P("tm", "gx", None, None)
    return jax.shard_map(shards, mesh=mesh, in_specs=in_specs, out_specs=out_specs, check_vma=False)
```

```python
import functools
import math

import jax
import jax.numpy as jnp
import numpy as np
from jax import lax
from jax.experimental import pallas as pl
from jax.experimental.pallas import tpu as pltpu
from jax.sharding import PartitionSpec as P


SWEEPS = 12
YHALO = 16
PAD = 8
GROUPS = 2
LIMIT = 24 * 1024 * 1024
COST = 5_000_000

cheb_centre = 1.0
cheb_half = 0.7

VMEM = pl.BlockSpec(memory_space=pltpu.VMEM)
SMEM = pl.BlockSpec(memory_space=pltpu.SMEM)


def omegas():
    return [
        1.0
        / (cheb_centre + cheb_half * math.cos(math.pi * (2 * turn + 1) / (2 * SWEEPS)))
        for turn in range(SWEEPS)
    ]


def mode_terms(total):
    time = np.arange(total)
    table = np.zeros((total, total))
    table[0] = 1.0
    table[1] = np.where(time % 2 == 0, 1.0, -1.0)
    for mode in range(1, total // 2):
        angle = 2.0 * np.pi * (mode * time % total) / total
        table[2 * mode] = np.cos(angle)
        table[2 * mode + 1] = -np.sin(angle)
    table[np.abs(table) < 1e-9] = 0.0
    return table


def weighted(values, weights):
    groups = {}
    for value, weight in zip(values, weights):
        size = round(abs(float(weight)), 12)
        if size == 0.0:
            continue
        sign = 1 if weight > 0 else -1
        groups.setdefault(size, []).append((sign, value))
    total = None
    for size, members in groups.items():
        sign, part = members[0]
        lead = sign
        for sign, value in members[1:]:
            part = part + value if sign == lead else part - value
        factor = lead * size
        if factor != 1.0:
            part = part * factor
        total = part if total is None else total + part
    return total


def spectra(values):
    total = len(values)
    half = total // 2
    table = mode_terms(total)
    even = [values[0]] + [values[n] + values[total - n] for n in range(1, half)] + [values[half]]
    odd = [values[n] - values[total - n] for n in range(1, half)]
    fields = [weighted(even, table[0][: half + 1]), weighted(even, table[1][: half + 1])]
    for mode in range(1, half):
        fields.append(weighted(even, table[2 * mode][: half + 1]))
        fields.append(weighted(odd, table[2 * mode + 1][1:half]))
    return fields


def near_sum(w_ref, lead, coef_ref, plane, row, shift=0):
    lanes = w_ref.shape[-1]
    at = pl.ds(row, 8)
    below = pl.ds(row - 1, 8)
    above = pl.ds(row + 1, 8)
    mine = plane - shift
    core = w_ref[lead, mine, at, :]
    face = coef_ref[2, plane, at, :]
    total = coef_ref[0, plane, at, :] * w_ref[lead, mine - 1, at, :]
    total = total + coef_ref[0, plane + 1, at, :] * w_ref[lead, mine + 1, at, :]
    total = total + coef_ref[1, plane, at, :] * w_ref[lead, mine, below, :]
    total = total + coef_ref[1, plane, above, :] * w_ref[lead, mine, above, :]
    total = total + face * pltpu.roll(core, 1, 1)
    total = total + pltpu.roll(face * core, lanes - 1, 1)
    return core, total


def sweep(source, target, coef_ref, w0_ref, inv_ref, omega, planes, chunks):
    first, count = planes

    def one(plane, chunk, pair):
        row = PAD + 8 * chunk
        at = pl.ds(8 * chunk, 8)
        a, b = 2 * pair, 2 * pair + 1
        core_a, sum_a = near_sum(source, a, coef_ref, plane, row)
        core_b, sum_b = near_sum(source, b, coef_ref, plane, row)
        inv_a = inv_ref[3 * pair, plane - 1, at, :]
        inv_b = inv_ref[3 * pair + 1, plane - 1, at, :]
        cross = inv_ref[3 * pair + 2, plane - 1, at, :]
        term_a = w0_ref[a, plane - 1, at, :] + (inv_a * sum_a - cross * sum_b)
        term_b = w0_ref[b, plane - 1, at, :] + (inv_b * sum_b + cross * sum_a)
        target[a, plane, pl.ds(row, 8), :] = (1.0 - omega) * core_a + omega * term_a
        target[b, plane, pl.ds(row, 8), :] = (1.0 - omega) * core_b + omega * term_b

    def two(turn, _):
        plane = first + 2 * turn
        for side in range(2):
            for chunk in chunks:
                for pair in range(source.shape[0] // 2):
                    one(plane + side, chunk, pair)
        return 0

    lax.fori_loop(0, count // 2, two, 0)


def chunks_of(rows, halo):
    first = (YHALO - halo) // 8
    return range(max(first, 0), min(rows // 8 - first, rows // 8))


def sweeps_on(buffers, coef_ref, w0_ref, inv_ref, done, block, rows):
    for step in range(block):
        reach = block - 1 - step
        sweep(
            buffers[step % 2],
            buffers[(step + 1) % 2],
            coef_ref,
            w0_ref,
            inv_ref,
            omegas()[done + step],
            (block - reach, block + 2 * reach),
            chunks_of(rows, SWEEPS - 1 - done - step),
        )
    return buffers[block % 2]


def load_in(buffer_a, parity, own_ref, on_ref, off_ref, window):
    block = own_ref.shape[1]
    at = pl.ds(PAD + window[0], window[1])
    first_on = jnp.where(parity == 0, 2 * block, 0)
    first_off = jnp.where(parity == 0, 0, 2 * block)

    def one(plane, _):
        for lead in range(own_ref.shape[0]):
            buffer_a[lead, block + plane, at, :] = own_ref[lead, plane]
            buffer_a[lead, first_on + plane, at, :] = on_ref[lead, plane]
            buffer_a[lead, first_off + plane, at, :] = off_ref[lead, plane]
        return 0

    lax.fori_loop(0, block, one, 0)


def clear_edges(refs, rows, depth):
    blank = jnp.zeros((PAD + depth, refs[0].shape[-1]), jnp.float32)

    def clear(plane, _):
        for ref in refs:
            for lead in range(ref.shape[0]):
                ref[lead, plane, pl.ds(0, PAD + depth), :] = blank
                ref[lead, plane, pl.ds(rows + PAD - depth, PAD + depth), :] = blank
        return 0

    lax.fori_loop(0, refs[0].shape[1], clear, 0)


def pack_kernel(chunk, weights_ref, state_ref, out_ref):
    step = pl.program_id(0)
    pieces, _, block, rows, lanes = out_ref.shape
    length = state_ref.shape[2]
    for plane in range(block):
        for piece in range(pieces):
            low = piece * chunk - YHALO
            first, last = max(low, 0), min(low + rows, length)
            if first > low:
                out_ref[piece, 0, plane, pl.ds(0, first - low), :] = jnp.zeros(
                    (first - low, lanes), jnp.float32
                )
            if last < low + rows:
                out_ref[piece, 0, plane, pl.ds(last - low, low + rows - last), :] = jnp.zeros(
                    (low + rows - last, lanes), jnp.float32
                )
            out_ref[piece, 0, plane, pl.ds(first - low, last - first), :] = state_ref[
                0, plane, pl.ds(first, last - first), :
            ]
    for piece in range(pieces):
        out_ref[piece, 0, 0, pl.ds(0, 1), :] = jnp.full((1, lanes), weights_ref[step], jnp.float32)


def finish_kernel(weights_ref, state_ref, back_ref, out_ref):
    pieces, steps, block, chunk, lanes = back_ref.shape
    for step in range(steps):
        weight = jnp.full((8, lanes), weights_ref[step], jnp.float32)
        scale = (1.0 / weight)[:1]
        for plane in range(block):
            for piece in range(pieces):
                at = pl.ds(piece * chunk, chunk)
                value = back_ref[piece, step, plane] * scale
                out_ref[step, plane, at, :] = state_ref[step, plane, at, :] + value


def residual_starts(wide, base, planes, state_own, field_of, coef_ref, diag_ref, inv_ref, w0_ref, w0_base):
    total = wide.shape[0]
    rows = diag_ref.shape[1]
    half = total // 2
    first, count = planes

    def one(turn, _):
        plane = first + turn
        for chunk in range(rows // 8):
            row = PAD + 8 * chunk
            at = pl.ds(8 * chunk, 8)
            around = diag_ref[plane - 1, at, :]
            values = []
            for lead in range(total):
                core, near = near_sum(wide, lead, coef_ref, plane, row, base)
                if lead == 0:
                    prior = field_of(plane, row)
                else:
                    prior = wide[lead - 1, plane - base, pl.ds(row, 8), :]
                value = prior - (around * core - near) - core * core * core
                values.append(value * state_own[lead, 0, pl.ds(0, 1), :])
            fields = spectra(values)
            for pair in range(half):
                spec_a, spec_b = fields[2 * pair], fields[2 * pair + 1]
                inv_a = inv_ref[3 * pair, plane - 1, at, :]
                inv_b = inv_ref[3 * pair + 1, plane - 1, at, :]
                cross = inv_ref[3 * pair + 2, plane - 1, at, :]
                w_a = inv_a * spec_a - cross * spec_b
                w_b = inv_b * spec_b + cross * spec_a
                w0_ref[2 * pair, plane - w0_base, at, :] = w_a
                w0_ref[2 * pair + 1, plane - w0_base, at, :] = w_b
        return 0

    lax.fori_loop(0, count, one, 0)


def edges_kernel(window, parity_ref, state_ref, on_ref, off_ref):
    block = state_ref.shape[1]
    near_on = jnp.where(parity_ref[0] == 0, block - 1, 0)

    def one(lead, _):
        on_ref[lead, 0] = state_ref[lead, near_on, pl.ds(*window), :]
        off_ref[lead, 0] = state_ref[lead, block - 1 - near_on, pl.ds(*window), :]
        return 0

    lax.fori_loop(0, state_ref.shape[0], one, 0)


def early_kernel(
    window,
    parity_ref,
    shift_real_ref,
    shift_imag_ref,
    state_own,
    state_on,
    fixed_own,
    fixed_on,
    fixed_off,
    coef_ref,
    diag_ref,
    inv_ref,
    w0_ref,
    wide,
    fixed,
):
    total, block, rows, lanes = state_own.shape
    half = total // 2
    planes = 3 * block
    parity = parity_ref[0]
    first_on = jnp.where(parity == 0, 2 * block, 0)
    first_off = jnp.where(parity == 0, 0, 2 * block)
    base = jnp.where(parity == 0, block, block - 1)
    clear_edges((fixed, coef_ref), rows, 0)
    clear_edges((wide,), rows, window[0])
    body = pl.ds(PAD, rows)
    for lead in range(total):
        at_on = jnp.where(parity == 0, block, 0)
        wide[lead, at_on, pl.ds(PAD + window[0], window[1]), :] = state_on[lead, 0]

    def place(plane, _):
        for lead in range(total):
            wide[lead, block - base + plane, body, :] = state_own[lead, plane]
        for lead in range(2):
            fixed[lead, block + plane, body, :] = fixed_own[lead, plane]
            fixed[lead, first_on + plane, body, :] = fixed_on[lead, plane]
            fixed[lead, first_off + plane, body, :] = fixed_off[lead, plane]
        return 0

    lax.fori_loop(0, block, place, 0)
    lane = lax.broadcasted_iota(jnp.int32, (8, lanes), 1)

    def faces(plane, _):
        for chunk in range(rows // 8):
            row = PAD + 8 * chunk
            at = pl.ds(row, 8)
            kappa = fixed[1, plane, at, :]
            coef_ref[0, plane, at, :] = 0.5 * (fixed[1, plane - 1, at, :] + kappa)
            coef_ref[1, plane, at, :] = 0.5 * (fixed[1, plane, pl.ds(row - 1, 8), :] + kappa)
            near = 0.5 * (pltpu.roll(kappa, 1, 1) + kappa)
            coef_ref[2, plane, at, :] = jnp.where(lane == 0, 0.0, near)
        return 0

    lax.fori_loop(1, planes, faces, 0)
    reals = [shift_real_ref[mode] for mode in range(half + 1)]
    imags = [shift_imag_ref[mode] for mode in range(half)]

    def inverses(plane, _):
        for chunk in range(rows // 8):
            row = PAD + 8 * chunk
            at = pl.ds(row, 8)
            out = pl.ds(8 * chunk, 8)
            kappa = fixed[1, plane, at, :]
            low = 0.5 * (kappa + jnp.where(lane == 0, 0.0, pltpu.roll(kappa, 1, 1)))
            high = 0.5 * (kappa + jnp.where(lane == lanes - 1, 0.0, pltpu.roll(kappa, lanes - 1, 1)))
            around = coef_ref[0, plane, at, :] + coef_ref[0, plane + 1, at, :]
            around = around + coef_ref[1, plane, at, :]
            around = around + coef_ref[1, plane, pl.ds(row + 1, 8), :]
            around = around + low + high
            diag_ref[plane - 1, out, :] = around
            inside = kappa > 0.0
            zero = jnp.zeros_like(kappa)
            inv_ref[0, plane - 1, out, :] = jnp.where(inside, 1.0 / (reals[0] + around), 0.0)
            inv_ref[1, plane - 1, out, :] = jnp.where(inside, 1.0 / (reals[half] + around), 0.0)
            inv_ref[2, plane - 1, out, :] = zero
            for mode in range(1, half):
                denom = reals[mode] + around
                scale = jnp.where(inside, 1.0 / (denom * denom + imags[mode] * imags[mode]), 0.0)
                value = denom * scale
                inv_ref[3 * mode, plane - 1, out, :] = value
                inv_ref[3 * mode + 1, plane - 1, out, :] = value
                inv_ref[3 * mode + 2, plane - 1, out, :] = -imags[mode] * scale
        return 0

    lax.fori_loop(1, planes - 1, inverses, 0)

    def field_of(plane, row):
        return fixed[0, plane, pl.ds(row, 8), :]

    first = jnp.where(parity == 0, block + 1, block)
    residual_starts(
        wide, base, (first, block - 1), state_own, field_of, coef_ref, diag_ref, inv_ref, w0_ref, block
    )


def late_kernel(
    window, parity_ref, state_own, state_off, fixed_own, coef_ref, diag_ref, inv_ref, w0_in, *rest
):
    w0_refs, wide, outer = rest[:-2], rest[-2], rest[-1]
    total, block, rows, _ = state_own.shape
    parity = parity_ref[0]
    base = jnp.where(parity == 0, block - 1, 2 * block - 2)
    at_off = jnp.where(parity == 0, 0, 2)
    at_own = jnp.where(parity == 0, 1, 0)
    from_own = jnp.where(parity == 0, 0, block - 2)
    clear_edges((wide,), rows, window[0])
    body = pl.ds(PAD, rows)
    for lead in range(total):
        wide[lead, at_off, pl.ds(PAD + window[0], window[1]), :] = state_off[lead, 0]
        wide[lead, at_own, body, :] = state_own[lead, from_own]
        wide[lead, at_own + 1, body, :] = state_own[lead, from_own + 1]

    def field_of(plane, row):
        return fixed_own[0, plane - block, pl.ds(row - PAD, 8), :]

    residual_starts(
        wide,
        base,
        (base + 1, 1),
        state_own,
        field_of,
        coef_ref,
        diag_ref,
        inv_ref,
        outer,
        base + 1,
    )
    inner = jnp.where(parity == 0, 1, 0)
    outermost = jnp.where(parity == 0, 0, block - 1)
    per = w0_refs[0].shape[0]
    at = pl.ds(*window)
    for group in range(len(w0_refs)):
        for lead in range(per):
            source = group * per + lead
            for plane in range(block - 1):
                w0_refs[group][lead, inner + plane] = w0_in[source, inner + plane, at, :]
            w0_refs[group][lead, outermost] = outer[source, 0, at, :]


def phase_kernel(
    low_pair, done, window, next_window, parity_ref, coef_ref, inv_ref, own_in, on_in, off_in, *rest
):
    buffer_a, buffer_b = rest[-2:]
    if done == 0:
        w0_ref, out_ref = rest[:2]
    else:
        w0_ref, out_ref = rest[0], rest[1]
    parity = parity_ref[0]
    pairs, block, rows = w0_ref.shape[0] // 2, own_in.shape[1], w0_ref.shape[2]
    group_inv = inv_ref.at[pl.ds(3 * low_pair, 3 * pairs)]
    load_in(buffer_a, parity, own_in, on_in, off_in, window)
    if done == 0:

        def keep(plane, _):
            for lead in range(2 * pairs):
                w0_ref[lead, plane] = buffer_a[lead, plane + 1, pl.ds(PAD, rows), :]
            return 0

        lax.fori_loop(0, w0_ref.shape[1], keep, 0)
    result = sweeps_on((buffer_a, buffer_b), coef_ref, w0_ref, group_inv, done, block, rows)
    at = pl.ds(PAD + next_window[0], next_window[1])

    def hand_on(plane, _):
        for lead in range(2 * pairs):
            out_ref[lead, plane] = result[lead, block + plane, at, :]
        return 0

    lax.fori_loop(0, block, hand_on, 0)


def last_kernel(low_pair, done, window, parity_ref, coef_ref, inv_ref, own_in, on_in, off_in, w0_ref, *rest):
    out_ref, buffer_a, buffer_b = rest[-3:]
    parity = parity_ref[0]
    pairs, block, rows = w0_ref.shape[0] // 2, own_in.shape[1], w0_ref.shape[2]
    total, chunk_rows = out_ref.shape[0], out_ref.shape[2]
    group_inv = inv_ref.at[pl.ds(3 * low_pair, 3 * pairs)]
    table = mode_terms(total).T / total
    table[:, 2:] *= 2.0
    load_in(buffer_a, parity, own_in, on_in, off_in, window)
    result = sweeps_on((buffer_a, buffer_b), coef_ref, w0_ref, group_inv, done, block, rows)

    def one(plane, _):
        for chunk in range(chunk_rows // 8):
            at = pl.ds(8 * chunk, 8)
            row = pl.ds(PAD + YHALO + 8 * chunk, 8)
            fields = [result[lead, block + plane, row, :] for lead in range(2 * pairs)]
            for lead in range(total):
                value = weighted(fields, table[lead, 2 * low_pair : 2 * (low_pair + pairs)])
                if len(rest) == 4:
                    value = value + rest[0][lead, plane, at, :]
                out_ref[lead, plane, at, :] = value
        return 0

    lax.fori_loop(0, block, one, 0)


def shards(state, start_field, diffusivity, time_weights, shift_real, shift_imag):
    steps, block, length, lanes = state.shape
    pieces = lax.axis_size("tm")
    slabs = lax.axis_size("gx")
    total = steps * pieces
    pairs = total // 2
    per = pairs // GROUPS
    chunk = length // pieces
    rows = chunk + 2 * YHALO
    planes = 3 * block
    padded = rows + 2 * PAD
    f32 = jnp.float32
    device = lax.axis_index("tm")
    parity = (lax.axis_index("gx") % 2).astype(jnp.int32).reshape((1,))
    on_pairs = [(i, i ^ 1) for i in range(slabs)]
    off_pairs = []
    for i in range(1, slabs - 1, 2):
        off_pairs += [(i, i + 1), (i + 1, i)]

    def shape(*dims):
        return jax.ShapeDtypeStruct(dims, f32)

    def swap_on(value):
        return lax.ppermute(value, "gx", on_pairs)

    def swap_off(value):
        return lax.ppermute(value, "gx", off_pairs)

    def call(kernel, inputs, scalars, outs, scratch, flops):
        return pl.pallas_call(
            kernel,
            in_specs=[SMEM] * scalars + [VMEM] * (len(inputs) - scalars),
            out_specs=[VMEM] * len(outs),
            out_shape=outs,
            scratch_shapes=[pltpu.VMEM(dims, f32) for dims in scratch],
            compiler_params=pltpu.CompilerParams(vmem_limit_bytes=LIMIT),
            cost_estimate=pl.CostEstimate(flops=flops, bytes_accessed=flops, transcendentals=0),
        )(*inputs)

    fixed = jnp.pad(jnp.stack([start_field, diffusivity]), ((0, 0), (0, 0), (YHALO, YHALO), (0, 0)))
    fixed = lax.dynamic_slice_in_dim(fixed, device * chunk, rows, axis=2)
    fixed_off = swap_off(fixed)
    fixed_on = swap_on(fixed)

    packed = pl.pallas_call(
        functools.partial(pack_kernel, chunk),
        grid=(steps,),
        in_specs=[SMEM, pl.BlockSpec((1, block, length, lanes), lambda i: (i, 0, 0, 0))],
        out_specs=pl.BlockSpec((pieces, 1, block, rows, lanes), lambda i: (0, i, 0, 0, 0)),
        out_shape=shape(pieces, steps, block, rows, lanes),
        name="pack",
    )(time_weights, state)
    mixed = lax.all_to_all(packed, "tm", split_axis=0, concat_axis=0, tiled=True)
    mixed = mixed.reshape((total, block, rows, lanes))
    windows = []
    for left in range(SWEEPS, 0, -block):
        low = (YHALO - left) // 4 * 4
        windows.append((low, rows - 2 * low))

    edge_kernel = functools.partial(edges_kernel, windows[0])
    edge = shape(total, 1, windows[0][1], lanes)
    edge_on, edge_off = call(edge_kernel, (parity, mixed), 1, [edge] * 2, [], COST // 10)
    mixed_off = swap_off(edge_off)
    mixed_on = swap_on(edge_on)

    coefs, diag, inverse, w0 = call(
        functools.partial(early_kernel, windows[0]),
        (parity, shift_real, shift_imag, mixed, mixed_on, fixed, fixed_on, fixed_off),
        3,
        [
            shape(3, planes, padded, lanes),
            shape(planes - 2, rows, lanes),
            shape(3 * pairs, planes - 2, rows, lanes),
            shape(total, block, rows, lanes),
        ],
        [(total, block + 1, padded, lanes), (2, planes, padded, lanes)],
        COST,
    )
    values = call(
        functools.partial(late_kernel, windows[0]),
        (parity, mixed, mixed_off, fixed, coefs, diag, inverse, w0),
        1,
        [shape(2 * per, block, windows[0][1], lanes)] * GROUPS,
        [(total, 3, padded, lanes), (total, 1, rows, lanes)],
        COST // 4,
    )
    buffers = [(2 * per, planes, padded, lanes)] * 2

    def exchange(value):
        return value, swap_on(value), swap_off(value)

    moving = [exchange(values[group]) for group in range(GROUPS)]
    starts = [None] * GROUPS
    last = len(windows) - 1
    for phase in range(last):
        for group in range(GROUPS):
            outs = [shape(2 * per, block, windows[phase + 1][1], lanes)]
            extra = ()
            if phase == 0:
                outs = [shape(2 * per, planes - 2, rows, lanes)] + outs
            else:
                extra = (starts[group],)
            results = call(
                functools.partial(
                    phase_kernel, per * group, block * phase, windows[phase], windows[phase + 1]
                ),
                (parity, coefs, inverse, *moving[group], *extra),
                1,
                outs,
                buffers,
                COST,
            )
            if phase == 0:
                starts[group] = results[0]
            moving[group] = exchange(results[-1])
    delta = ()
    for group in range(GROUPS):
        delta = call(
            functools.partial(last_kernel, per * group, block * last, windows[last]),
            (parity, coefs, inverse, *moving[group], starts[group], *delta),
            1,
            [shape(total, block, chunk, lanes)],
            buffers,
            COST,
        )
    back = lax.all_to_all(
        delta[0].reshape((pieces, steps, block, chunk, lanes)),
        "tm",
        split_axis=0,
        concat_axis=0,
        tiled=True,
    )
    out = shape(steps, block, length, lanes)
    return call(finish_kernel, (time_weights, state, back), 1, [out], [], COST // 3)[0]


def solution(mesh):
    in_specs = (
        P("tm", "gx", None, None),
        P("gx", None, None),
        P("gx", None, None),
        P("tm"),
        P(),
        P(),
    )
    out_specs = P("tm", "gx", None, None)
    return jax.shard_map(shards, mesh=mesh, in_specs=in_specs, out_specs=out_specs, check_vma=False)
```
